512 devices in a mesh: req: 128 (over y_lo, z, x, core), tp: 4 (over y_hi).
Axes of the slice: x: 4, y: 8 (y_hi: 4, y_lo: 2; y = y_hi * 2 + y_lo), z: 8, core: 2. Of those that a mesh axis runs over, the one named last changes fastest.
Arguments:
- hidden: bfloat16 [128, 128, 2048], P('req', None, 'tp'), may hold values from -600 to 600
- norm_gain: bfloat16 [2048], replicated, may hold values from 0.099609375 to 1.8984375
- w_query: bfloat16 [2048, 2048], P('req', 'tp'), may hold values from -0.125 to 0.125
- w_key: bfloat16 [2048, 512], P('req', 'tp'), may hold values from -0.125 to 0.125
- w_value: bfloat16 [2048, 512], P('req', 'tp'), may hold values from -0.125 to 0.125
- w_out: bfloat16 [2048, 2048], P('tp', 'req'), may hold values from -0.125 to 0.125
- cache_keys: bfloat16 [128, 2048, 512], P('req', None, 'tp'), may hold values from -72 to 72
- cache_values: bfloat16 [128, 2048, 512], P('req', None, 'tp'), may hold values from -6 to 6
- cache_lengths: int32 [128], replicated, may hold values from 1 to 2048, 131072 in all
Outputs:
- attn_out: bfloat16 [128, 128, 2048], P('req', None, 'tp')
- new_keys: bfloat16 [128, 128, 512], P('req', None, 'tp')
- new_values: bfloat16 [128, 128, 512], P('req', None, 'tp')
The draws below stay inside these ranges and needn't reach their ends.
Inputs may be any that keep to these rules, and one draw needn't show every extreme that they name: `cache_lengths`: one request has exactly 2048 cached positions; all requests together have 128 * 1024.
All inputs are finite; a program needn't handle non-finite values.
Results may differ from the reference program's by a relative error of at most 0.015.
Values may be sent and summed in bfloat16 or wider, within the bound.
A program may use at most 64 MiB of HBM per device.

```python
import math
import jax
import jax.numpy as jnp
import numpy as np
from jax import lax

D = 2048
HEADS = 32
KVH = 8
HD = 64
TOK_DEV = 128
CACHE = 2048
REQS = 128
N_TP = 4


def draw_hidden(key, part):
    key_base, key_rows, key_cols = jax.random.split(key, 3)
    shape_full = (REQS, TOK_DEV, D)
    row_scale = jnp.exp(jax.random.uniform(key_rows, (REQS, TOK_DEV, 1), jnp.float32, 0.0, math.log(10.0)))
    col_scale = jnp.exp(jax.random.uniform(key_cols, (1, 1, D), jnp.float32, 0.0, math.log(10.0)))
    base_draw = jnp.clip(jax.random.normal(key_base, shape_full, jnp.float32), -6.0, 6.0)
    return (base_draw * row_scale * col_scale).astype(jnp.bfloat16)


def draw_cache_keys(key, part):
    key_base = jax.random.fold_in(key, 0)
    shape_full = (REQS, CACHE, KVH * HD)
    result_draw = jnp.clip(jax.random.normal(key_base, shape_full, jnp.float32), -4.0, 4.0)
    return result_draw.astype(jnp.bfloat16)


def block_scale(stream_key, shape, shards, low, top_value):
    level, own = 1.0, jax.random.fold_in(stream_key, 6)
    for position, parts in shards:
        draws = jnp.exp(jax.random.uniform(jax.random.fold_in(own, position), (parts,), jnp.float32, low / len(shards), top_value / len(shards)))
        level = level * jnp.repeat(draws, shape[position] // parts).reshape([-1 if axis == position else 1 for axis in range(len(shape))])
    return level


def profile(count, total, most, skew):
    portions = [(1 << 20) // math.isqrt(standing ** skew) + 1 for standing in range(2, count + 1)]
    spare, counts = total - most - (count - 1), [1] * (count - 1)
    while spare > 0:
        movable = [i for i in range(count - 1) if counts[i] < most]
        pool, budget = sum([portions[i] for i in movable]), spare
        for i in movable:
            extra = min(most - counts[i], max(1, budget * portions[i] // pool), spare)
            counts[i] = counts[i] + extra
            spare = spare - extra
    return np.array([most] + counts)


def uneven(key, amount, total, most, slope):
    if amount == 2:
        one = jax.random.randint(key, (), max(1, total - most), min(most, total - 1) + 1)
        return jnp.stack([one, total - one])
    sizes = jnp.asarray(profile(amount, total, most, slope), jnp.int32)
    twos = (amount - 1) // 2
    giver, taker = sizes[1:1 + 2 * twos:2], sizes[2:2 + 2 * twos:2]
    room = jnp.minimum(giver - 1, most - taker)
    passed = jax.random.randint(jax.random.fold_in(key, 1), (twos,), 0, 1 << 20) % (room + 1)
    sizes = sizes.at[1:1 + 2 * twos:2].set(giver - passed).at[2:2 + 2 * twos:2].set(taker + passed)
    return sizes[jax.random.permutation(jax.random.fold_in(key, 2), amount)]


def noise(key, extent, spread, bound, cuts=(), kind=jnp.bfloat16):
    factor_of = block_scale(key, extent, cuts, -0.22, 0.18) if cuts else 1.0
    values = jax.random.normal(key, extent, jnp.float32) * spread * factor_of
    return jnp.minimum(jnp.maximum(values, -bound), bound).astype(kind)


def setup_inputs(seed: int = 0) -> dict:
    key_of = jax.random.split(jax.random.key(seed), 10)
    hidden = draw_hidden(jax.random.fold_in(key_of[9], 71), 0)
    norm_gain = jnp.clip(1.0 + 0.18 * jax.random.normal(key_of[1], (D,), jnp.float32), 0.099609375, 1.8984375).astype(jnp.bfloat16)
    w_query = noise(key_of[2], (D, HEADS * HD), D ** -0.5, 0.125, ((0, 128), (1, 4)))
    w_key = noise(key_of[3], (D, KVH * HD), D ** -0.5, 0.125, ((0, 128), (1, 4)))
    w_value = noise(key_of[4], (D, KVH * HD), D ** -0.5, 0.125, ((0, 128), (1, 4)))
    w_out = noise(key_of[5], (HEADS * HD, D), (HEADS * HD) ** -0.5, 0.125, ((0, 4), (1, 128)))
    cache_keys = draw_cache_keys(jax.random.fold_in(key_of[9], 71), 0)
    cache_values = noise(key_of[7], (REQS, CACHE, KVH * HD), 1.0, 6.0, ((0, 128), (2, 4)))
    cache_lengths = uneven(key_of[8], REQS, REQS * CACHE // 2, CACHE, 2).astype(jnp.int32)
    return {"hidden": hidden, "norm_gain": norm_gain, "w_query": w_query, "w_key": w_key, "w_value": w_value, "w_out": w_out, "cache_keys": cache_keys, "cache_values": cache_values, "cache_lengths": cache_lengths}


rope_base = 1000000.0
norm_eps = 1e-05

def rotate(tensor, cosine_table, sine_table):
    half_width = tensor.shape[-1] // 2
    front_half = tensor[..., :half_width]
    back_half = tensor[..., half_width:]
    return jnp.concatenate([front_half * cosine_table - back_half * sine_table, back_half * cosine_table + front_half * sine_table], axis=-1)

def phases(length_now, row_count):
    positions = (length_now + jnp.arange(row_count, dtype=jnp.int32)).astype(jnp.float32)
    inverse = rope_base ** (-jnp.arange(0, HD, 2, dtype=jnp.int32).astype(jnp.float32) / HD)
    phase_grid = positions[:, None] * inverse[None, :]
    return (jnp.cos(phase_grid)[:, None, :], jnp.sin(phase_grid)[:, None, :])

def one_request(hidden_rows, key_cache, value_cache, length_now, norm_gain, w_query, w_key, w_value, w_out):
    as_float = hidden_rows.astype(jnp.float32)
    mean_square = lax.optimization_barrier(jnp.mean(as_float * as_float, axis=-1, keepdims=True))
    normed = (as_float * lax.rsqrt(mean_square + norm_eps) * norm_gain.astype(jnp.float32)).astype(jnp.bfloat16)
    query_rows = jnp.dot(normed, w_query, preferred_element_type=jnp.float32).reshape(TOK_DEV, HEADS, HD)
    key_rows = jnp.dot(normed, w_key, preferred_element_type=jnp.float32).reshape(TOK_DEV, KVH, HD)
    value_rows = jnp.dot(normed, w_value, preferred_element_type=jnp.float32).reshape(TOK_DEV, KVH, HD)
    cosine_table, sine_table = phases(length_now, TOK_DEV)
    queries = rotate(query_rows, cosine_table, sine_table).astype(jnp.bfloat16)
    new_keys = rotate(key_rows, cosine_table, sine_table).astype(jnp.bfloat16)
    new_values = value_rows.astype(jnp.bfloat16)
    all_keys = jnp.concatenate([key_cache.reshape(CACHE, KVH, HD), new_keys], axis=0)
    all_values = jnp.concatenate([value_cache.reshape(CACHE, KVH, HD), new_values], axis=0)
    grouped = queries.reshape(TOK_DEV, KVH, HEADS // KVH, HD)
    scores = jnp.einsum('tkgd,skd->kgts', grouped.astype(jnp.float32), all_keys.astype(jnp.float32)) * HD ** (-0.5)
    slot_index = jnp.arange(CACHE + TOK_DEV, dtype=jnp.int32)
    token_index = jnp.arange(TOK_DEV, dtype=jnp.int32)
    visible = jnp.where(slot_index[None, :] < CACHE, slot_index[None, :] < length_now, slot_index[None, :] - CACHE <= token_index[:, None])
    scores = jnp.where(visible[None, None], scores, -jnp.inf)
    row_peak = lax.optimization_barrier(jnp.max(scores, axis=-1, keepdims=True))
    weights = jnp.exp(scores - row_peak)
    probabilities = (weights / lax.optimization_barrier(jnp.sum(weights, axis=-1, keepdims=True))).astype(jnp.bfloat16)
    mixed_heads = jnp.einsum('kgts,skd->tkgd', probabilities.astype(jnp.float32), all_values.astype(jnp.float32))
    mixed_heads = mixed_heads.astype(jnp.bfloat16).reshape(TOK_DEV, HEADS * HD)
    group_rows = HEADS * HD // N_TP
    out_sum = jnp.zeros((TOK_DEV, D), jnp.float32)
    for head_group in range(N_TP):
        term = jnp.dot(mixed_heads[:, head_group * group_rows:(head_group + 1) * group_rows], w_out[head_group * group_rows:(head_group + 1) * group_rows], preferred_element_type=jnp.float32)
        rounded = lax.optimization_barrier(term.astype(jnp.bfloat16))
        out_sum = out_sum + rounded.astype(jnp.float32)
    return (out_sum.astype(jnp.bfloat16), new_keys.reshape(TOK_DEV, KVH * HD), new_values.reshape(TOK_DEV, KVH * HD))

def reference(hidden, norm_gain, w_query, w_key, w_value, w_out, cache_keys, cache_values, cache_lengths):

    def per_request(request_items):
        return one_request(request_items[0], request_items[1], request_items[2], request_items[3], norm_gain, w_query, w_key, w_value, w_out)
    results = lax.map(per_request, (hidden, cache_keys, cache_values, cache_lengths))
    return (results[0], results[1], results[2])
```

```python
import functools

import jax
import jax.numpy as jnp
from jax import lax
from jax.experimental import pallas as pl
from jax.experimental.pallas import tpu as pltpu
from jax.sharding import PartitionSpec as P

HD = 64
NY, NZ, NX = 2, 8, 4
N_TP = 4
TOK = 128
ROW_BLOCKS = 4

rope_base = 1000000.0
norm_eps = 1e-05
masked_score = -1e30
MESH = pl.DeviceIdType.MESH


def ring_keys(axis, n):
    keys = []
    for s in range(1, n // 2 + 1):
        for u in (0, 1):
            for d in (1, -1):
                if s < n // 2 or (u == 0) == (d == 1):
                    keys.append((axis, d, s, u))
    return keys


RING = {"x": ring_keys("x", NX), "z": ring_keys("z", NZ)}
SIZE = {"x": NX, "z": NZ}
STAGES = {0: ("x", "z"), 1: ("z", "x")}
PASS = {c: [("own", 0), ("own", 1)] + RING[STAGES[c][1]] for c in (0, 1)}
KEYS = (
    ["local", "core", "y"]
    + RING["x"]
    + RING["z"]
    + [("pass", c) + (k,) for c in (0, 1) for k in PASS[c]]
)
KEY_INDEX = {k: i for i, k in enumerate(KEYS)}


class Place:
    def __init__(self):
        req = lax.axis_index("req")
        self.tp = lax.axis_index("tp")
        self.core = lax.rem(req, 2)
        self.x = lax.rem(lax.div(req, 2), NX)
        self.z = lax.rem(lax.div(req, 2 * NX), NZ)
        self.y = lax.div(req, 2 * NX * NZ)

    def device(self, core=None, x=None, z=None, y=None, tp=None):
        core = self.core if core is None else core
        x = self.x if x is None else x
        z = self.z if z is None else z
        y = self.y if y is None else y
        tp = self.tp if tp is None else tp
        return (((y * NZ + z) * NX + x) * 2 + core, tp)

    def along(self, axis, offset):
        n = SIZE[axis]
        here = self.x if axis == "x" else self.z
        return lax.rem(here + (offset + 2 * n), n)


class Gather:
    def __init__(self, place, loc, buf, send, recv):
        self.place, self.loc, self.buf, self.send, self.recv = place, loc, buf, send, recv

    def first_block(self, c, u, axis, o):
        p = self.place
        yu = p.y if u == 0 else 1 - p.y
        return self.buf.at[c, yu, p.z, o] if axis == "x" else self.buf.at[c, yu, o, p.x]

    def second_block(self, c, u, axis, o):
        p = self.place
        yu = p.y if u == 0 else 1 - p.y
        return self.buf.at[c, yu, o] if axis == "z" else self.buf.at[c, yu, :, o]

    def make(self, c, key):
        p, i = self.place, KEY_INDEX[key]
        if key == "local":
            return pltpu.make_async_copy(
                self.loc.at[c], self.buf.at[c, p.y, p.z, p.x, pl.ds(c * 16, 16)], self.send.at[i]
            )
        if key == "core":
            src = self.loc.at[1 - c]
            dst = self.buf.at[1 - c, p.y, p.z, p.x, pl.ds(c * 16, 16)]
            dev = p.device(core=1 - p.core)
        elif key == "y":
            src = dst = self.buf.at[c, p.y, p.z, p.x]
            dev = p.device(y=1 - p.y)
        elif key[0] == "pass":
            axis = STAGES[c][1]
            if key[2][0] == "own":
                u, o = key[2][1], p.along(axis, 0)
            else:
                _, d, s, u = key[2]
                o = p.along(axis, -d * s)
            src = dst = self.second_block(c, u, axis, o)
            dev = p.device(core=1 - p.core)
        else:
            axis, d, s, u = key
            o = p.along(axis, -d * (s - 1))
            pick = self.first_block if STAGES[c][0] == axis else self.second_block
            src = dst = pick(c, u, axis, o)
            dev = p.device(**{axis: p.along(axis, d)})
        return pltpu.make_async_remote_copy(
            src_ref=src,
            dst_ref=dst,
            send_sem=self.send.at[i],
            recv_sem=self.recv.at[i],
            device_id=dev,
            device_id_type=MESH,
        )

    def start(self, c, key):
        self.make(c, key).start()

    def land(self, c, key):
        self.make(c, key).wait_recv()

    def steps(self, c):
        first, second = STAGES[c]
        out = []

        def begin():
            self.start(c, "core")
            self.start(c, "local")

        def own():
            self.make(c, "local").wait()
            self.land(c, "core")
            for d in (1, -1):
                self.start(c, (first, d, 1, 0))
            self.start(c, "y")

        def other():
            self.land(c, "y")
            for d in (1, -1):
                self.start(c, (first, d, 1, 1))

        def enter_second(u):
            for d in (1, -1):
                self.start(c, (second, d, 1, u))
            self.start(c, ("pass", c, ("own", u)))

        def first_step(s):
            last = s == SIZE[first] // 2
            for key in RING[first]:
                _, d, ks, u = key
                if ks == s:
                    self.land(c, key)
                    if last:
                        enter_second(u)
                    elif (first, d, s + 1, u) in KEY_INDEX:
                        self.start(c, (first, d, s + 1, u))

        def second_step(s):
            for key in RING[second]:
                _, d, ks, u = key
                if ks == s:
                    self.land(c, key)
                    if (second, d, s + 1, u) in KEY_INDEX:
                        self.start(c, (second, d, s + 1, u))
                    self.start(c, ("pass", c, key))

        def finish():
            for k in PASS[1 - c]:
                self.land(1 - c, ("pass", 1 - c, k))
            for k in ["core", "y"] + RING["x"] + RING["z"]:
                self.make(c, k).wait_send()
            for k in PASS[c]:
                self.make(c, ("pass", c, k)).wait_send()

        out += [begin, own, other]
        out += [functools.partial(first_step, s) for s in range(1, SIZE[first] // 2 + 1)]
        out += [functools.partial(second_step, s) for s in range(1, SIZE[second] // 2 + 1)]
        out += [finish]
        return out


N_STEPS = 3 + NX // 2 + NZ // 2 + 1


def rotate(tile, cosine, sine, lane):
    partner = jnp.where((lane % 64) < 32, pltpu.roll(tile, 96, 1), pltpu.roll(tile, 32, 1))
    return tile * cosine + partner * sine


def kernel(
    lengths,
    hidden,
    gain,
    loc_in,
    loc_out,
    cosine,
    sine,
    keys,
    values,
    out,
    new_keys,
    new_values,
    rows,
    buf_in,
    buf_out,
    normed,
    queries,
    mixed_blocks,
    terms,
    landed,
    send_in,
    recv_in,
    send_out,
    recv_out,
    send_tp,
    recv_tp,
):
    place = Place()
    barrier = pltpu.get_barrier_semaphore()
    partners = [place.device(core=1 - place.core), place.device(y=1 - place.y)]
    for axis in ("x", "z"):
        partners += [place.device(**{axis: place.along(axis, d)}) for d in (1, -1)]
    others = [lax.rem(place.tp + d, N_TP) for d in range(N_TP)]
    partners += [place.device(tp=others[d]) for d in range(1, N_TP)]
    for partner in partners:
        pl.semaphore_signal(barrier, inc=1, device_id=partner, device_id_type=MESH)
    pl.semaphore_wait(barrier, len(partners))

    gather_in = Gather(place, loc_in, buf_in, send_in, recv_in)
    gather_out = Gather(place, loc_out, buf_out, send_out, recv_out)
    steps_in = {c: gather_in.steps(c) for c in (0, 1)}
    steps_out = {c: gather_out.steps(c) for c in (0, 1)}

    def run(steps, i):
        for c in (0, 1):
            pl.when(place.core == c)(steps[c][i])

    def hidden_copy(d):
        return pltpu.make_async_remote_copy(
            src_ref=hidden,
            dst_ref=rows.at[place.tp],
            send_sem=send_tp.at[d],
            recv_sem=recv_tp.at[d],
            device_id=place.device(tp=others[d]),
            device_id_type=MESH,
        )

    own_rows = pltpu.make_async_copy(hidden, rows.at[place.tp], send_tp.at[0])

    run(steps_in, 0)
    for d in (2, 1, 3):
        hidden_copy(d).start()
    own_rows.start()
    run(steps_out, 0)
    run(steps_in, 1)
    run(steps_in, 2)
    run(steps_out, 1)
    run(steps_in, 3)
    run(steps_out, 2)
    run(steps_in, 4)

    own_rows.wait()
    for d in (1, 2, 3):
        hidden_copy(d).wait()
    squares = 0.0
    for j in range(N_TP):
        part = rows[j].astype(jnp.float32)
        squares += jnp.sum(part * part, axis=-1, keepdims=True)
    scale = lax.rsqrt(squares * (1.0 / (512 * N_TP)) + norm_eps)
    for j in range(N_TP):
        part = rows[j].astype(jnp.float32)
        normed[j] = (part * scale * gain[:, 512 * j : 512 * (j + 1)].astype(jnp.float32)).astype(
            jnp.bfloat16
        )

    for i in range(5, N_STEPS - 1):
        run(steps_in, i)
    run(steps_out, 3)
    run(steps_in, N_STEPS - 1)

    def project(c):
        total = jnp.zeros((TOK, 384), jnp.float32)
        for j in range(N_TP):
            block = buf_in[c, j // 2, 4 * (j % 2) : 4 * (j % 2) + 4].reshape(512, 384)
            total += jnp.dot(normed[j], block, preferred_element_type=jnp.float32)
        return total

    first, second = project(0), project(1)
    lane = lax.broadcasted_iota(jnp.int32, (TOK, 128), 1)
    low = lane < 64
    cos_table, sin_table = cosine[...], sine[...]
    fresh_keys = rotate(first[:, 256:], cos_table, sin_table, lane).astype(jnp.bfloat16)
    fresh_values = second[:, 256:].astype(jnp.bfloat16)
    new_keys[...] = fresh_keys
    new_values[...] = fresh_values
    for g, half in enumerate((first, second)):
        for pair in range(2):
            tile = rotate(half[:, 128 * pair : 128 * pair + 128], cos_table, sin_table, lane)
            tile = tile.astype(jnp.bfloat16).astype(jnp.float32) * (HD**-0.5)
            swapped = pltpu.roll(tile, 64, 1)
            if g == 0:
                heads = (jnp.where(low, tile, 0.0), jnp.where(low, swapped, 0.0))
            else:
                heads = (jnp.where(low, 0.0, swapped), jnp.where(low, 0.0, tile))
            for k in range(2):
                queries[2 * g + pair, 128 * k : 128 * k + 128, :] = heads[k].astype(jnp.bfloat16)

    length = lengths[lax.axis_index("req")]
    slot = lax.broadcasted_iota(jnp.int32, (1, 2048), 1)
    cache_bias = jnp.where(slot < length, 0.0, masked_score)
    row_token = lax.broadcasted_iota(jnp.int32, (2 * TOK, TOK), 0) % TOK
    new_bias = jnp.where(
        lax.broadcasted_iota(jnp.int32, (2 * TOK, TOK), 1) <= row_token, 0.0, masked_score
    )
    contract_last = (((1,), (1,)), ((), ()))

    def attend(i, carry):
        for k in range(ROW_BLOCKS):

            @pl.when(i == k)
            def _():
                run(steps_out, 4 + k)

        block = queries[i]
        cache_scores = (
            lax.dot_general(block, keys[...], contract_last, preferred_element_type=jnp.float32)
            + cache_bias
        )
        new_scores = (
            lax.dot_general(
                block, new_keys[...], contract_last, preferred_element_type=jnp.float32
            )
            + new_bias
        )
        peak = jnp.maximum(
            jnp.max(cache_scores, axis=-1, keepdims=True),
            jnp.max(new_scores, axis=-1, keepdims=True),
        )
        cache_weights = jnp.exp(cache_scores - peak)
        new_weights = jnp.exp(new_scores - peak)
        total = jnp.sum(cache_weights, axis=-1, keepdims=True) + jnp.sum(
            new_weights, axis=-1, keepdims=True
        )
        mixed = jnp.dot(
            cache_weights.astype(jnp.bfloat16), values[...], preferred_element_type=jnp.float32
        ) + jnp.dot(
            new_weights.astype(jnp.bfloat16), new_values[...], preferred_element_type=jnp.float32
        )
        mixed_blocks[i] = mixed / total
        return carry

    lax.fori_loop(0, ROW_BLOCKS, attend, 0)

    for i in range(8, N_STEPS):
        run(steps_out, i)

    halves = []
    for g in range(2):
        tiles = []
        for pair in range(2):
            even = mixed_blocks[2 * g + pair, :TOK, :]
            odd = mixed_blocks[2 * g + pair, TOK:, :]
            if g == 0:
                tile = jnp.where(low, even, pltpu.roll(odd, 64, 1))
            else:
                tile = jnp.where(low, pltpu.roll(even, 64, 1), odd)
            tiles.append(tile.astype(jnp.bfloat16))
        halves.append(jnp.concatenate(tiles, axis=1))

    def term_copy(d):
        return pltpu.make_async_remote_copy(
            src_ref=terms.at[d - 1],
            dst_ref=landed.at[d - 1],
            send_sem=send_tp.at[3 + d],
            recv_sem=recv_tp.at[3 + d],
            device_id=place.device(tp=others[d]),
            device_id_type=MESH,
        )

    def term(d):
        target = others[d]
        total = jnp.zeros((TOK, 512), jnp.float32)
        for c in range(2):
            block = buf_out[c, lax.div(target, 2), pl.ds(4 * lax.rem(target, 2), 4)]
            total += lax.dot_general(
                halves[c],
                block.reshape(512, 256),
                contract_last,
                preferred_element_type=jnp.float32,
            )
        return total.astype(jnp.bfloat16)

    for d in (2, 1, 3):
        terms[d - 1] = term(d)
        term_copy(d).start()
    summed = term(0).astype(jnp.float32)
    for d in (1, 3, 2):
        term_copy(d).wait()
        summed += landed[d - 1].astype(jnp.float32)
    out[...] = summed.astype(jnp.bfloat16)


def per_device(
    hidden, norm_gain, w_query, w_key, w_value, w_out, cache_keys, cache_values, cache_lengths
):
    length = cache_lengths[lax.axis_index("req")]
    positions = (length + jnp.arange(TOK, dtype=jnp.int32)).astype(jnp.float32)
    inverse = rope_base ** (-jnp.arange(0, HD, 2, dtype=jnp.int32).astype(jnp.float32) / HD)
    phase = positions[:, None] * inverse[None, :]
    cosine, sine = jnp.cos(phase), jnp.sin(phase)
    cosine = jnp.concatenate([cosine] * 4, axis=1)
    sine = jnp.concatenate([-sine, sine] * 2, axis=1)
    loc_in = jnp.stack(
        [
            jnp.concatenate([w_query[:, :256], w_key], axis=1),
            jnp.concatenate([w_query[:, 256:], w_value], axis=1),
        ]
    )
    loc_out = w_out.T.reshape(16, 2, 256).transpose(1, 0, 2)
    vmem = pl.BlockSpec(memory_space=pltpu.VMEM)
    bf16, f32 = jnp.bfloat16, jnp.float32
    n_keys = len(KEYS)
    results = pl.pallas_call(
        kernel,
        out_shape=(
            jax.ShapeDtypeStruct((TOK, 512), bf16),
            jax.ShapeDtypeStruct((TOK, 128), bf16),
            jax.ShapeDtypeStruct((TOK, 128), bf16),
        ),
        in_specs=[pl.BlockSpec(memory_space=pltpu.SMEM)] + [vmem] * 8,
        out_specs=(vmem, vmem, vmem),
        scratch_shapes=[
            pltpu.VMEM((N_TP, TOK, 512), bf16),
            pltpu.VMEM((2, NY, NZ, NX, 32, 384), bf16),
            pltpu.VMEM((2, NY, NZ, NX, 32, 256), bf16),
            pltpu.VMEM((N_TP, TOK, 512), bf16),
            pltpu.VMEM((ROW_BLOCKS, 2 * TOK, 128), bf16),
            pltpu.VMEM((ROW_BLOCKS, 2 * TOK, 128), f32),
            pltpu.VMEM((N_TP - 1, TOK, 512), bf16),
            pltpu.VMEM((N_TP - 1, TOK, 512), bf16),
            pltpu.SemaphoreType.DMA((n_keys,)),
            pltpu.SemaphoreType.DMA((n_keys,)),
            pltpu.SemaphoreType.DMA((n_keys,)),
            pltpu.SemaphoreType.DMA((n_keys,)),
            pltpu.SemaphoreType.DMA((7,)),
            pltpu.SemaphoreType.DMA((7,)),
        ],
        compiler_params=pltpu.CompilerParams(
            collective_id=0, has_side_effects=True, vmem_limit_bytes=56 * 1024 * 1024
        ),
    )(
        cache_lengths,
        hidden[0],
        norm_gain.reshape(1, -1),
        loc_in,
        loc_out,
        cosine,
        sine,
        cache_keys[0],
        cache_values[0],
    )
    return tuple(r[None] for r in results)


def solution(mesh):
    in_specs = (
        P("req", None, "tp"),
        P(),
        P("req", "tp"),
        P("req", "tp"),
        P("req", "tp"),
        P("tp", "req"),
        P("req", None, "tp"),
        P("req", None, "tp"),
        P(),
    )
    out_specs = (P("req", None, "tp"), P("req", None, "tp"), P("req", None, "tp"))
    return jax.shard_map(
        per_device, mesh=mesh, in_specs=in_specs, out_specs=out_specs, check_vma=False
    )
```

```python
import functools

import jax
import jax.numpy as jnp
import numpy as np
from jax import lax
from jax.experimental import pallas as pl
from jax.experimental.pallas import tpu as pltpu
from jax.sharding import PartitionSpec as P

HD = 64
NY, NZ, NX = 2, 8, 4
N_TP = 4
TOK = 128
ROW_BLOCKS = 4

rope_base = 1000000.0
norm_eps = 1e-05
masked_score = -1e30
MESH = pl.DeviceIdType.MESH


def ring_keys(axis, n):
    keys = []
    for s in range(1, n // 2 + 1):
        for u in (0, 1):
            for d in (1, -1):
                if s < n // 2 or (u == 0) == (d == 1):
                    keys.append((axis, d, s, u))
    return keys


SIZE = {"x": NX, "z": NZ}
RING = {a: ring_keys(a, SIZE[a]) for a in SIZE}
DIRECT = {
    a: [
        ("direct", a, k, u)
        for u in (0, 1)
        for k in sorted(range(1, SIZE[a]), key=lambda k: -min(k, SIZE[a] - k))
    ]
    for a in SIZE
}
STAGES = {0: ("x", "z"), 1: ("z", "x")}
PASS = {c: [("own", 0), ("own", 1)] + RING[STAGES[c][1]] for c in (0, 1)}
KEYS = (
    [("local", 0), ("local", 1), ("core", 0), ("core", 1), "y"]
    + RING["x"]
    + RING["z"]
    + DIRECT["x"]
    + DIRECT["z"]
    + [("pass", c) + (k,) for c in (0, 1) for k in PASS[c]]
)
KEY_INDEX = {k: i for i, k in enumerate(KEYS)}


class Place:
    def __init__(self):
        req = lax.axis_index("req")
        self.tp = lax.axis_index("tp")
        self.core = lax.rem(req, 2)
        self.x = lax.rem(lax.div(req, 2), NX)
        self.z = lax.rem(lax.div(req, 2 * NX), NZ)
        self.y = lax.div(req, 2 * NX * NZ)

    def device(self, core=None, x=None, z=None, y=None, tp=None):
        core = self.core if core is None else core
        x = self.x if x is None else x
        z = self.z if z is None else z
        y = self.y if y is None else y
        tp = self.tp if tp is None else tp
        return (((y * NZ + z) * NX + x) * 2 + core, tp)

    def along(self, axis, offset):
        n = SIZE[axis]
        here = self.x if axis == "x" else self.z
        return lax.rem(here + (offset + 2 * n), n)


class Gather:
    def __init__(self, place, parts, buf, send, recv):
        self.place, self.parts, self.buf, self.send, self.recv = place, parts, buf, send, recv

    def first_block(self, c, u, axis, o):
        p = self.place
        yu = p.y if u == 0 else 1 - p.y
        return self.buf.at[c, yu, p.z, o] if axis == "x" else self.buf.at[c, yu, o, p.x]

    def second_block(self, c, u, axis, o):
        p = self.place
        yu = p.y if u == 0 else 1 - p.y
        return self.buf.at[c, yu, o] if axis == "z" else self.buf.at[c, yu, :, o]

    def make(self, c, key):
        p, i = self.place, KEY_INDEX[key]
        if key[0] == "local":
            src, column = self.parts[c][key[1]]
            columns = pl.ds(column, src.shape[1])
            dst = self.buf.at[c, p.y, p.z, p.x, pl.ds(c * 16, 16), columns]
            return pltpu.make_async_copy(src, dst, self.send.at[i])
        if key[0] == "core":
            src, column = self.parts[1 - c][key[1]]
            columns = pl.ds(column, src.shape[1])
            dst = self.buf.at[1 - c, p.y, p.z, p.x, pl.ds(c * 16, 16), columns]
            dev = p.device(core=1 - p.core)
        elif key == "y":
            src = dst = self.buf.at[c, p.y, p.z, p.x]
            dev = p.device(y=1 - p.y)
        elif key[0] == "pass":
            axis = STAGES[c][1]
            if key[2][0] == "own":
                u, o = key[2][1], p.along(axis, 0)
            else:
                _, d, s, u = key[2]
                o = p.along(axis, -d * s)
            src = dst = self.second_block(c, u, axis, o)
            dev = p.device(core=1 - p.core)
        elif key[0] == "direct":
            _, axis, k, u = key
            src = dst = self.first_block(c, u, axis, p.along(axis, 0))
            dev = p.device(**{axis: p.along(axis, k)})
        else:
            axis, d, s, u = key
            src = dst = self.second_block(c, u, axis, p.along(axis, -d * (s - 1)))
            dev = p.device(**{axis: p.along(axis, d)})
        return pltpu.make_async_remote_copy(
            src_ref=src,
            dst_ref=dst,
            send_sem=self.send.at[i],
            recv_sem=self.recv.at[i],
            device_id=dev,
            device_id_type=MESH,
        )

    def start(self, c, key):
        self.make(c, key).start()

    def land(self, c, key):
        self.make(c, key).wait_recv()

    def steps(self, c):
        first, second = STAGES[c]
        n_parts = range(len(self.parts[c]))

        def begin():
            for k in n_parts:
                self.start(c, ("core", k))
            for k in n_parts:
                self.start(c, ("local", k))

        def own():
            for k in n_parts:
                self.make(c, ("local", k)).wait()
                self.arrive(c, k)
            self.start(c, "y")
            for key in DIRECT[first]:
                if key[3] == 0:
                    self.start(c, key)

        def other():
            self.land(c, "y")
            for key in DIRECT[first]:
                if key[3] == 1:
                    self.start(c, key)

        def enter_second():
            for u in (0, 1):
                for key in DIRECT[first]:
                    if key[3] == u:
                        self.land(c, key)
                for d in (1, -1):
                    self.start(c, (second, d, 1, u))
                self.start(c, ("pass", c, ("own", u)))

        def ring_step(keys):
            for key in keys:
                _, d, s, u = key
                self.land(c, key)
                if (second, d, s + 1, u) in KEY_INDEX:
                    self.start(c, (second, d, s + 1, u))
                self.start(c, ("pass", c, key))

        def finish():
            for k in PASS[1 - c]:
                self.land(1 - c, ("pass", 1 - c, k))
            sent = [("core", k) for k in n_parts] + ["y"] + DIRECT[first] + RING[second]
            for k in sent + [("pass", c, k) for k in PASS[c]]:
                self.make(c, k).wait_send()

        count = RING_STEPS
        size = -(-len(RING[second]) // count)
        chunks = [RING[second][i * size : (i + 1) * size] for i in range(count)]
        return (
            [begin, own, other, enter_second]
            + [functools.partial(ring_step, chunk) for chunk in chunks]
            + [finish]
        )

    def arrive(self, c, k):
        self.make(1 - c, ("core", k)).wait_recv()


RING_STEPS = 4


def rotate(tile, cosine, sine, lane):
    partner = jnp.where((lane % 64) < 32, pltpu.roll(tile, 96, 1), pltpu.roll(tile, 32, 1))
    return tile * cosine + partner * sine


def kernel(
    lengths,
    hidden,
    gain,
    inverse,
    w_query,
    w_key,
    w_value,
    w_out,
    keys_far,
    values_far,
    out,
    new_keys,
    new_values,
    rows,
    keys,
    values,
    buf_in,
    buf_out,
    normed,
    queries,
    mixed_blocks,
    terms,
    landed,
    cosine,
    sine,
    send_in,
    recv_in,
    send_out,
    recv_out,
    send_tp,
    recv_tp,
    cache_sem,
):
    place = Place()
    cache_copies = [
        pltpu.make_async_copy(keys_far, keys, cache_sem.at[0]),
        pltpu.make_async_copy(values_far, values, cache_sem.at[1]),
    ]
    barrier = pltpu.get_barrier_semaphore()
    partners = [place.device(core=1 - place.core), place.device(y=1 - place.y)]
    for axis in ("x", "z"):
        partners += [
            place.device(**{axis: place.along(axis, k)}) for k in range(1, SIZE[axis])
        ]
    others = [lax.rem(place.tp + d, N_TP) for d in range(N_TP)]
    partners += [place.device(tp=others[d]) for d in range(1, N_TP)]
    for partner in partners:
        pl.semaphore_signal(barrier, inc=1, device_id=partner, device_id_type=MESH)
    for copy in cache_copies:
        copy.start()

    lane = lax.broadcasted_iota(jnp.int32, (TOK, 128), 1)
    position = lengths[lax.axis_index("req")] + lax.broadcasted_iota(jnp.int32, (TOK, 128), 0)
    phase = position.astype(jnp.float32) * inverse[...]
    cosine[...] = jnp.cos(phase)
    sine[...] = jnp.where((lane % 64) < 32, -1.0, 1.0) * jnp.sin(phase)

    pl.semaphore_wait(barrier, len(partners))

    parts_in = [
        [(w_query.at[:, pl.ds(256 * half, 256)], 0), ((w_key, w_value)[half], 256)]
        for half in (0, 1)
    ]
    parts_out = [[(w_out.at[:, pl.ds(256 * half, 256)], 0)] for half in (0, 1)]
    gather_in = Gather(place, parts_in, buf_in, send_in, recv_in)
    gather_out = Gather(place, parts_out, buf_out, send_out, recv_out)
    steps_in = {c: gather_in.steps(c) for c in (0, 1)}
    steps_out = {c: gather_out.steps(c) for c in (0, 1)}

    def run(steps, i):
        for c in (0, 1):
            pl.when(place.core == c)(steps[c][i])

    def hidden_copy(d):
        return pltpu.make_async_remote_copy(
            src_ref=hidden,
            dst_ref=rows.at[place.tp],
            send_sem=send_tp.at[d],
            recv_sem=recv_tp.at[d],
            device_id=place.device(tp=others[d]),
            device_id_type=MESH,
        )

    own_rows = pltpu.make_async_copy(hidden, rows.at[place.tp], send_tp.at[0])

    run(steps_in, 0)
    own_rows.start()
    run(steps_out, 0)
    run(steps_in, 1)
    run(steps_out, 1)
    for d in (2, 1, 3):
        hidden_copy(d).start()
    run(steps_in, 2)
    run(steps_out, 2)
    run(steps_in, 3)
    run(steps_in, 4)
    run(steps_in, 5)
    run(steps_out, 3)
    run(steps_in, 6)
    run(steps_in, 7)

    own_rows.wait()
    for d in (1, 2, 3):
        hidden_copy(d).wait()
    squares = 0.0
    for j in range(N_TP):
        part = rows[j].astype(jnp.float32)
        squares += jnp.sum(part * part, axis=-1, keepdims=True)
    scale = lax.rsqrt(squares * (1.0 / (512 * N_TP)) + norm_eps)
    for j in range(N_TP):
        part = rows[j].astype(jnp.float32)
        normed[j] = (part * scale * gain[:, 512 * j : 512 * (j + 1)].astype(jnp.float32)).astype(
            jnp.bfloat16
        )

    run(steps_in, 8)
    run(steps_out, 4)

    def project(c):
        total = jnp.zeros((TOK, 384), jnp.float32)
        for j in range(N_TP):
            block = buf_in[c, j // 2, 4 * (j % 2) : 4 * (j % 2) + 4].reshape(512, 384)
            total += jnp.dot(normed[j], block, preferred_element_type=jnp.float32)
        return total

    first, second = project(0), project(1)
    low = lane < 64
    cos_table, sin_table = cosine[...], sine[...]
    fresh_keys = rotate(first[:, 256:], cos_table, sin_table, lane).astype(jnp.bfloat16)
    fresh_values = second[:, 256:].astype(jnp.bfloat16)
    new_keys[...] = fresh_keys
    new_values[...] = fresh_values
    for g, half in enumerate((first, second)):
        for pair in range(2):
            tile = rotate(half[:, 128 * pair : 128 * pair + 128], cos_table, sin_table, lane)
            tile = tile.astype(jnp.bfloat16).astype(jnp.float32) * (HD**-0.5)
            swapped = pltpu.roll(tile, 64, 1)
            if g == 0:
                heads = (jnp.where(low, tile, 0.0), jnp.where(low, swapped, 0.0))
            else:
                heads = (jnp.where(low, 0.0, swapped), jnp.where(low, 0.0, tile))
            for k in range(2):
                queries[2 * g + pair, 128 * k : 128 * k + 128, :] = heads[k].astype(jnp.bfloat16)

    length = lengths[lax.axis_index("req")]
    slot = lax.broadcasted_iota(jnp.int32, (1, 2048), 1)
    cache_bias = jnp.where(slot < length, 0.0, masked_score)
    row_token = lax.broadcasted_iota(jnp.int32, (2 * TOK, TOK), 0) % TOK
    new_bias = jnp.where(
        lax.broadcasted_iota(jnp.int32, (2 * TOK, TOK), 1) <= row_token, 0.0, masked_score
    )
    contract_last = (((1,), (1,)), ((), ()))

    def attend(i, carry):
        for k in range(3):

            @pl.when(i == k)
            def _():
                run(steps_out, 5 + k)

        block = queries[i]
        cache_scores = (
            lax.dot_general(block, keys[...], contract_last, preferred_element_type=jnp.float32)
            + cache_bias
        )
        new_scores = (
            lax.dot_general(
                block, new_keys[...], contract_last, preferred_element_type=jnp.float32
            )
            + new_bias
        )
        peak = jnp.maximum(
            jnp.max(cache_scores, axis=-1, keepdims=True),
            jnp.max(new_scores, axis=-1, keepdims=True),
        )
        cache_weights = jnp.exp(cache_scores - peak)
        new_weights = jnp.exp(new_scores - peak)
        total = jnp.sum(cache_weights, axis=-1, keepdims=True) + jnp.sum(
            new_weights, axis=-1, keepdims=True
        )
        mixed = jnp.dot(
            cache_weights.astype(jnp.bfloat16), values[...], preferred_element_type=jnp.float32
        ) + jnp.dot(
            new_weights.astype(jnp.bfloat16), new_values[...], preferred_element_type=jnp.float32
        )
        mixed_blocks[i] = mixed / total
        return carry

    for copy in cache_copies:
        copy.wait()
    lax.fori_loop(0, ROW_BLOCKS, attend, 0)

    run(steps_out, 8)

    halves = []
    for g in range(2):
        tiles = []
        for pair in range(2):
            even = mixed_blocks[2 * g + pair, :TOK, :]
            odd = mixed_blocks[2 * g + pair, TOK:, :]
            if g == 0:
                tile = jnp.where(low, even, pltpu.roll(odd, 64, 1))
            else:
                tile = jnp.where(low, pltpu.roll(even, 64, 1), odd)
            tiles.append(tile.astype(jnp.bfloat16))
        halves.append(jnp.concatenate(tiles, axis=1))

    def term_copy(d):
        return pltpu.make_async_remote_copy(
            src_ref=terms.at[d - 1],
            dst_ref=landed.at[d - 1],
            send_sem=send_tp.at[3 + d],
            recv_sem=recv_tp.at[3 + d],
            device_id=place.device(tp=others[d]),
            device_id_type=MESH,
        )

    def term(d):
        target = others[d]
        total = jnp.zeros((TOK, 512), jnp.float32)
        for c in range(2):
            block = buf_out[c, lax.div(target, 2), pl.ds(4 * lax.rem(target, 2), 4)]
            total += lax.dot_general(
                halves[c],
                block.reshape(512, 256),
                contract_last,
                preferred_element_type=jnp.float32,
            )
        return total.astype(jnp.bfloat16)

    for d in (2, 1, 3):
        terms[d - 1] = term(d)
        term_copy(d).start()
    summed = term(0).astype(jnp.float32)
    for d in (1, 3, 2):
        term_copy(d).wait()
        summed += landed[d - 1].astype(jnp.float32)
    out[...] = summed.astype(jnp.bfloat16)


def per_device(
    hidden, norm_gain, w_query, w_key, w_value, w_out, cache_keys, cache_values, cache_lengths
):
    powers = np.arange(0, HD, 2, dtype=np.float64) / HD
    inverse = np.tile((rope_base**-powers).astype(np.float32), 4).reshape(1, 128)
    vmem = pl.BlockSpec(memory_space=pltpu.VMEM)
    far = pl.BlockSpec(memory_space=pl.ANY)
    bf16, f32 = jnp.bfloat16, jnp.float32
    n_keys = len(KEYS)
    results = pl.pallas_call(
        kernel,
        out_shape=(
            jax.ShapeDtypeStruct((TOK, 512), bf16),
            jax.ShapeDtypeStruct((TOK, 128), bf16),
            jax.ShapeDtypeStruct((TOK, 128), bf16),
        ),
        in_specs=[pl.BlockSpec(memory_space=pltpu.SMEM), far, vmem, vmem] + [far] * 6,
        out_specs=(vmem, vmem, vmem),
        scratch_shapes=[
            pltpu.VMEM((N_TP, TOK, 512), bf16),
            pltpu.VMEM((2048, 128), bf16),
            pltpu.VMEM((2048, 128), bf16),
            pltpu.VMEM((2, NY, NZ, NX, 32, 384), bf16),
            pltpu.VMEM((2, NY, NZ, NX, 32, 256), bf16),
            pltpu.VMEM((N_TP, TOK, 512), bf16),
            pltpu.VMEM((ROW_BLOCKS, 2 * TOK, 128), bf16),
            pltpu.VMEM((ROW_BLOCKS, 2 * TOK, 128), f32),
            pltpu.VMEM((N_TP - 1, TOK, 512), bf16),
            pltpu.VMEM((N_TP - 1, TOK, 512), bf16),
            pltpu.VMEM((TOK, 128), f32),
            pltpu.VMEM((TOK, 128), f32),
            pltpu.SemaphoreType.DMA((n_keys,)),
            pltpu.SemaphoreType.DMA((n_keys,)),
            pltpu.SemaphoreType.DMA((n_keys,)),
            pltpu.SemaphoreType.DMA((n_keys,)),
            pltpu.SemaphoreType.DMA((7,)),
            pltpu.SemaphoreType.DMA((7,)),
            pltpu.SemaphoreType.DMA((2,)),
        ],
        compiler_params=pltpu.CompilerParams(
            collective_id=0, has_side_effects=True, vmem_limit_bytes=56 * 1024 * 1024
        ),
    )(
        cache_lengths,
        hidden[0],
        norm_gain.reshape(1, -1),
        jnp.asarray(inverse),
        w_query,
        w_key,
        w_value,
        w_out.T,
        cache_keys[0],
        cache_values[0],
    )
    return tuple(r[None] for r in results)


def solution(mesh):
    in_specs = (
        P("req", None, "tp"),
        P(),
        P("req", "tp"),
        P("req", "tp"),
        P("req", "tp"),
        P("tp", "req"),
        P("req", None, "tp"),
        P("req", None, "tp"),
        P(),
    )
    out_specs = (P("req", None, "tp"), P("req", None, "tp"), P("req", None, "tp"))
    return jax.shard_map(
        per_device, mesh=mesh, in_specs=in_specs, out_specs=out_specs, check_vma=False
    )
```

```python
import functools

import jax
import jax.numpy as jnp
import numpy as np
from jax import lax
from jax.experimental import pallas as pl
from jax.experimental.pallas import tpu as pltpu
from jax.sharding import PartitionSpec as P

HD = 64
NY, NZ, NX = 2, 8, 4
N_TP = 4
TOK = 128
ROW_BLOCKS = 4
HALF = TOK // 2

rope_base = 1000000.0
norm_eps = 1e-05
masked_score = -1e30
MESH = pl.DeviceIdType.MESH


def ring_keys(axis, n):
    keys = []
    for s in range(1, n // 2 + 1):
        for u in (0, 1):
            for d in (1, -1):
                if s < n // 2 or (u == 0) == (d == 1):
                    keys.append((axis, d, s, u))
    return keys


SIZE = {"x": NX, "z": NZ}
RING = {a: ring_keys(a, SIZE[a]) for a in SIZE}
DIRECT = {"x": [("direct", "x", k, u) for u in (0, 1) for k in (2, 1, 3)]}
STAGES = {0: ("x", "z"), 1: ("z", "x")}
FIRST = {"x": DIRECT["x"], "z": RING["z"]}
PASS = {c: [("own", 0), ("own", 1)] + RING[STAGES[c][1]] for c in (0, 1)}
KEYS = (
    [("local", 0), ("local", 1), ("core", 0), ("core", 1), "y"]
    + RING["x"]
    + RING["z"]
    + DIRECT["x"]
    + [("pass", c) + (k,) for c in (0, 1) for k in PASS[c]]
)
KEY_INDEX = {k: i for i, k in enumerate(KEYS)}


class Place:
    def __init__(self):
        req = lax.axis_index("req")
        self.tp = lax.axis_index("tp")
        self.core = lax.rem(req, 2)
        self.x = lax.rem(lax.div(req, 2), NX)
        self.z = lax.rem(lax.div(req, 2 * NX), NZ)
        self.y = lax.div(req, 2 * NX * NZ)

    def device(self, core=None, x=None, z=None, y=None, tp=None):
        core = self.core if core is None else core
        x = self.x if x is None else x
        z = self.z if z is None else z
        y = self.y if y is None else y
        tp = self.tp if tp is None else tp
        return (((y * NZ + z) * NX + x) * 2 + core, tp)

    def along(self, axis, offset):
        n = SIZE[axis]
        here = self.x if axis == "x" else self.z
        return lax.rem(here + (offset + 2 * n), n)


class Gather:
    def __init__(self, place, parts, buf, send, recv):
        self.place, self.parts, self.buf, self.send, self.recv = place, parts, buf, send, recv

    def first_block(self, c, u, axis, o):
        p = self.place
        yu = p.y if u == 0 else 1 - p.y
        return self.buf[c].at[yu, p.z, o] if axis == "x" else self.buf[c].at[yu, o, p.x]

    def second_block(self, c, u, axis, o):
        p = self.place
        yu = p.y if u == 0 else 1 - p.y
        return self.buf[c].at[yu, o] if axis == "z" else self.buf[c].at[yu, :, o]

    def make(self, c, key):
        p, i = self.place, KEY_INDEX[key]
        if key[0] == "local":
            src, column = self.parts[c][key[1]]
            columns = pl.ds(column, src.shape[1])
            dst = self.buf[c].at[p.y, p.z, p.x, pl.ds(c * 16, 16), columns]
            return pltpu.make_async_copy(src, dst, self.send.at[i])
        if key[0] == "core":
            src, column = self.parts[1 - c][key[1]]
            columns = pl.ds(column, src.shape[1])
            dst = self.buf[1 - c].at[p.y, p.z, p.x, pl.ds(c * 16, 16), columns]
            dev = p.device(core=1 - p.core)
        elif key == "y":
            src = dst = self.buf[c].at[p.y, p.z, p.x]
            dev = p.device(y=1 - p.y)
        elif key[0] == "pass":
            axis = STAGES[c][1]
            if key[2][0] == "own":
                u, o = key[2][1], p.along(axis, 0)
            else:
                _, d, s, u = key[2]
                o = p.along(axis, -d * s)
            src = dst = self.second_block(c, u, axis, o)
            dev = p.device(core=1 - p.core)
        elif key[0] == "direct":
            _, axis, k, u = key
            src = dst = self.first_block(c, u, axis, p.along(axis, 0))
            dev = p.device(**{axis: p.along(axis, k)})
        else:
            axis, d, s, u = key
            pick = self.first_block if axis == STAGES[c][0] else self.second_block
            src = dst = pick(c, u, axis, p.along(axis, -d * (s - 1)))
            dev = p.device(**{axis: p.along(axis, d)})
        return pltpu.make_async_remote_copy(
            src_ref=src,
            dst_ref=dst,
            send_sem=self.send.at[i],
            recv_sem=self.recv.at[i],
            device_id=dev,
            device_id_type=MESH,
        )

    def start(self, c, key):
        self.make(c, key).start()

    def land(self, c, key):
        self.make(c, key).wait_recv()

    def steps(self, c):
        first, second = STAGES[c]
        n_parts = range(len(self.parts[c]))

        def begin():
            for k in n_parts:
                self.start(c, ("core", k))
            for k in n_parts:
                self.start(c, ("local", k))

        def start_first(u):
            for key in FIRST[first]:
                if key[3] == u and (key[0] == "direct" or key[2] == 1):
                    self.start(c, key)

        def own():
            for k in n_parts:
                self.make(c, ("local", k)).wait()
                self.arrive(c, k)
            self.start(c, "y")
            start_first(0)

        def other():
            self.land(c, "y")
            start_first(1)

        def enter_second(u):
            for d in (1, -1):
                self.start(c, (second, d, 1, u))
            self.start(c, ("pass", c, ("own", u)))

        def after_direct():
            for u in (0, 1):
                for key in DIRECT[first]:
                    if key[3] == u:
                        self.land(c, key)
                enter_second(u)

        def first_step(step):
            for key in RING[first]:
                _, d, s, u = key
                if s == step:
                    self.land(c, key)
                    if s == SIZE[first] // 2:
                        enter_second(u)
                    elif (first, d, s + 1, u) in KEY_INDEX:
                        self.start(c, (first, d, s + 1, u))

        def ring_step(keys):
            for key in keys:
                _, d, s, u = key
                self.land(c, key)
                if (second, d, s + 1, u) in KEY_INDEX:
                    self.start(c, (second, d, s + 1, u))
                self.start(c, ("pass", c, key))

        def finish():
            for k in PASS[1 - c]:
                self.land(1 - c, ("pass", 1 - c, k))
            sent = [("core", k) for k in n_parts] + ["y"] + FIRST[first] + RING[second]
            for k in sent + [("pass", c, k) for k in PASS[c]]:
                self.make(c, k).wait_send()

        if first == "x":
            middle = [after_direct]
        else:
            middle = [functools.partial(first_step, i) for i in range(1, SIZE[first] // 2 + 1)]
        for i in range(1, SIZE[second] // 2 + 1):
            middle.append(functools.partial(ring_step, [k for k in RING[second] if k[2] == i]))
        middle += [lambda: None] * (6 - len(middle))
        return [begin, own, other] + middle + [finish]

    def arrive(self, c, k):
        self.make(1 - c, ("core", k)).wait_recv()


def rotate(tile, cosine, sine, lane):
    partner = jnp.where((lane % 64) < 32, pltpu.roll(tile, 96, 1), pltpu.roll(tile, 32, 1))
    return tile * cosine + partner * sine


def kernel(
    lengths,
    hidden,
    gain,
    inverse,
    w_query,
    w_key,
    w_value,
    w_out,
    keys_far,
    values_far,
    out,
    new_keys,
    new_values,
    rows,
    keys,
    values,
    buf_in_0,
    buf_in_1,
    buf_out_0,
    buf_out_1,
    normed,
    queries,
    mixed_blocks,
    terms,
    landed,
    cosine,
    sine,
    send_in,
    recv_in,
    send_out,
    recv_out,
    send_tp,
    recv_tp,
    cache_sem,
):
    place = Place()
    cache_copies = [
        pltpu.make_async_copy(keys_far, keys, cache_sem.at[0]),
        pltpu.make_async_copy(values_far, values, cache_sem.at[1]),
    ]
    barrier = pltpu.get_barrier_semaphore()
    partners = [place.device(core=1 - place.core), place.device(y=1 - place.y)]
    for axis in ("x", "z"):
        partners += [
            place.device(**{axis: place.along(axis, k)})
            for k in range(1, SIZE[axis])
            if axis == "x" or k in (1, SIZE[axis] - 1)
        ]
    others = [lax.rem(place.tp + d, N_TP) for d in range(N_TP)]
    partners += [place.device(tp=others[d]) for d in range(1, N_TP)]
    for partner in partners:
        pl.semaphore_signal(barrier, inc=1, device_id=partner, device_id_type=MESH)
    for copy in cache_copies:
        copy.start()

    lane = lax.broadcasted_iota(jnp.int32, (TOK, 128), 1)
    position = lengths[lax.axis_index("req")] + lax.broadcasted_iota(jnp.int32, (TOK, 128), 0)
    phase = position.astype(jnp.float32) * inverse[...]
    cosine[...] = jnp.cos(phase)
    sine[...] = jnp.where((lane % 64) < 32, -1.0, 1.0) * jnp.sin(phase)

    pl.semaphore_wait(barrier, len(partners))

    parts_in = [
        [(w_query.at[:, pl.ds(256 * half, 256)], 0), ((w_key, w_value)[half], 256)]
        for half in (0, 1)
    ]
    parts_out = [[(w_out.at[:, pl.ds(0, 128)], 0)], [(w_out.at[:, pl.ds(128, 384)], 0)]]
    buf_in, buf_out = (buf_in_0, buf_in_1), (buf_out_0, buf_out_1)
    gather_in = Gather(place, parts_in, buf_in, send_in, recv_in)
    gather_out = Gather(place, parts_out, buf_out, send_out, recv_out)
    steps_in = {c: gather_in.steps(c) for c in (0, 1)}
    steps_out = {c: gather_out.steps(c) for c in (0, 1)}

    def run(steps, i):
        for c in (0, 1):
            pl.when(place.core == c)(steps[c][i])

    def hidden_copy(d):
        return pltpu.make_async_remote_copy(
            src_ref=hidden,
            dst_ref=rows.at[place.tp],
            send_sem=send_tp.at[d],
            recv_sem=recv_tp.at[d],
            device_id=place.device(tp=others[d]),
            device_id_type=MESH,
        )

    own_rows = pltpu.make_async_copy(hidden, rows.at[place.tp], send_tp.at[0])

    run(steps_in, 0)
    own_rows.start()
    run(steps_out, 0)
    run(steps_in, 1)
    run(steps_in, 2)
    run(steps_out, 1)
    for d in (2, 1, 3):
        hidden_copy(d).start()
    run(steps_in, 3)
    run(steps_out, 2)
    run(steps_in, 4)
    run(steps_out, 3)
    run(steps_in, 5)
    run(steps_out, 4)
    run(steps_in, 6)
    run(steps_out, 5)
    run(steps_in, 7)
    run(steps_out, 6)
    run(steps_in, 8)
    run(steps_out, 7)

    own_rows.wait()
    for d in (1, 2, 3):
        hidden_copy(d).wait()
    squares = 0.0
    for j in range(N_TP):
        part = rows[j].astype(jnp.float32)
        squares += jnp.sum(part * part, axis=-1, keepdims=True)
    scale = lax.rsqrt(squares * (1.0 / (512 * N_TP)) + norm_eps)
    for j in range(N_TP):
        part = rows[j].astype(jnp.float32)
        normed[j] = (part * scale * gain[:, 512 * j : 512 * (j + 1)].astype(jnp.float32)).astype(
            jnp.bfloat16
        )

    run(steps_in, 9)

    def project(c):
        total = jnp.zeros((TOK, 384), jnp.float32)
        for j in range(N_TP):
            block = buf_in[c][j // 2, 4 * (j % 2) : 4 * (j % 2) + 4].reshape(512, 384)
            total += jnp.dot(normed[j], block, preferred_element_type=jnp.float32)
        return total

    first, second = project(0), project(1)
    low = lane < 64
    cos_table, sin_table = cosine[...], sine[...]
    fresh_keys = rotate(first[:, 256:], cos_table, sin_table, lane).astype(jnp.bfloat16)
    fresh_values = second[:, 256:].astype(jnp.bfloat16)
    new_keys[...] = fresh_keys
    new_values[...] = fresh_values
    for g, half in enumerate((first, second)):
        for pair in range(2):
            tile = rotate(half[:, 128 * pair : 128 * pair + 128], cos_table, sin_table, lane)
            tile = tile.astype(jnp.bfloat16).astype(jnp.float32) * (HD**-0.5)
            swapped = pltpu.roll(tile, 64, 1)
            if g == 0:
                heads = (jnp.where(low, tile, 0.0), jnp.where(low, swapped, 0.0))
            else:
                heads = (jnp.where(low, 0.0, swapped), jnp.where(low, 0.0, tile))
            for k in range(2):
                head = heads[k].astype(jnp.bfloat16)
                row = HALF * (2 * pair + k)
                for t in range(2):
                    queries[2 * t + g, row : row + HALF, :] = head[HALF * t : HALF * (t + 1)]

    length = lengths[lax.axis_index("req")]
    slot = lax.broadcasted_iota(jnp.int32, (1, 2048), 1)
    cache_bias = jnp.where(slot < length, 0.0, masked_score)
    row_token = lax.broadcasted_iota(jnp.int32, (2 * TOK, TOK), 0) % HALF
    new_slot = lax.broadcasted_iota(jnp.int32, (2 * TOK, TOK), 1)
    contract_last = (((1,), (1,)), ((), ()))

    def attend(i, carry):
        pl.when(i == 0)(lambda: run(steps_out, 8))
        block = queries[i]
        cache_scores = (
            lax.dot_general(block, keys[...], contract_last, preferred_element_type=jnp.float32)
            + cache_bias
        )
        new_scores = (
            lax.dot_general(
                block, new_keys[...], contract_last, preferred_element_type=jnp.float32
            )
            + jnp.where(new_slot <= row_token + HALF * lax.div(i, 2), 0.0, masked_score)
        )
        peak = jnp.maximum(
            jnp.max(cache_scores, axis=-1, keepdims=True),
            jnp.max(new_scores, axis=-1, keepdims=True),
        )
        cache_weights = jnp.exp(cache_scores - peak)
        new_weights = jnp.exp(new_scores - peak)
        total = jnp.sum(cache_weights, axis=-1, keepdims=True) + jnp.sum(
            new_weights, axis=-1, keepdims=True
        )
        mixed = jnp.dot(
            cache_weights.astype(jnp.bfloat16), values[...], preferred_element_type=jnp.float32
        ) + jnp.dot(
            new_weights.astype(jnp.bfloat16), new_values[...], preferred_element_type=jnp.float32
        )
        mixed_blocks[i] = mixed / total
        return carry

    for copy in cache_copies:
        copy.wait()
    low = lax.broadcasted_iota(jnp.int32, (HALF, 128), 1) < 64

    def mixed_rows(t):
        tiles = []
        for g in range(2):
            for pair in range(2):
                row = 2 * HALF * pair
                even = mixed_blocks[2 * t + g, row : row + HALF, :]
                odd = mixed_blocks[2 * t + g, row + HALF : row + 2 * HALF, :]
                if g == 0:
                    tile = jnp.where(low, even, pltpu.roll(odd, 64, 1))
                else:
                    tile = jnp.where(low, pltpu.roll(even, 64, 1), odd)
                tiles.append(tile.astype(jnp.bfloat16))
        return tiles[0], jnp.concatenate(tiles[1:], axis=1)

    def term_copy(t, d):
        return pltpu.make_async_remote_copy(
            src_ref=terms.at[d - 1, pl.ds(HALF * t, HALF)],
            dst_ref=landed.at[d - 1, pl.ds(HALF * t, HALF)],
            send_sem=send_tp.at[1 + 3 * (t + 1) + d - 1],
            recv_sem=recv_tp.at[1 + 3 * (t + 1) + d - 1],
            device_id=place.device(tp=others[d]),
            device_id_type=MESH,
        )

    def term(shares, d):
        target = others[d]
        total = jnp.zeros((HALF, 512), jnp.float32)
        for c in range(2):
            block = buf_out[c][lax.div(target, 2), pl.ds(4 * lax.rem(target, 2), 4)]
            total += lax.dot_general(
                shares[c],
                block.reshape(512, block.shape[-1]),
                contract_last,
                preferred_element_type=jnp.float32,
            )
        return total.astype(jnp.bfloat16)

    own_terms = []
    for t in range(2):
        lax.fori_loop(2 * t, 2 * t + 2, attend, 0)
        if t == 0:
            run(steps_out, 9)
        shares = mixed_rows(t)
        for d in (2, 1, 3):
            terms[d - 1, HALF * t : HALF * (t + 1), :] = term(shares, d)
            term_copy(t, d).start()
        own_terms.append(term(shares, 0).astype(jnp.float32))
    for t in range(2):
        summed = own_terms[t]
        for d in (1, 3, 2):
            term_copy(t, d).wait()
            summed += landed[d - 1, HALF * t : HALF * (t + 1), :].astype(jnp.float32)
        out[HALF * t : HALF * (t + 1), :] = summed.astype(jnp.bfloat16)


def per_device(
    hidden, norm_gain, w_query, w_key, w_value, w_out, cache_keys, cache_values, cache_lengths
):
    powers = np.arange(0, HD, 2, dtype=np.float64) / HD
    inverse = np.tile((rope_base**-powers).astype(np.float32), 4).reshape(1, 128)
    vmem = pl.BlockSpec(memory_space=pltpu.VMEM)
    far = pl.BlockSpec(memory_space=pl.ANY)
    bf16, f32 = jnp.bfloat16, jnp.float32
    n_keys = len(KEYS)
    results = pl.pallas_call(
        kernel,
        out_shape=(
            jax.ShapeDtypeStruct((TOK, 512), bf16),
            jax.ShapeDtypeStruct((TOK, 128), bf16),
            jax.ShapeDtypeStruct((TOK, 128), bf16),
        ),
        in_specs=[pl.BlockSpec(memory_space=pltpu.SMEM), far, vmem, vmem] + [far] * 6,
        out_specs=(vmem, vmem, vmem),
        scratch_shapes=[
            pltpu.VMEM((N_TP, TOK, 512), bf16),
            pltpu.VMEM((2048, 128), bf16),
            pltpu.VMEM((2048, 128), bf16),
            pltpu.VMEM((NY, NZ, NX, 32, 384), bf16),
            pltpu.VMEM((NY, NZ, NX, 32, 384), bf16),
            pltpu.VMEM((NY, NZ, NX, 32, 128), bf16),
            pltpu.VMEM((NY, NZ, NX, 32, 384), bf16),
            pltpu.VMEM((N_TP, TOK, 512), bf16),
            pltpu.VMEM((ROW_BLOCKS, 2 * TOK, 128), bf16),
            pltpu.VMEM((ROW_BLOCKS, 2 * TOK, 128), f32),
            pltpu.VMEM((N_TP - 1, TOK, 512), bf16),
            pltpu.VMEM((N_TP - 1, TOK, 512), bf16),
            pltpu.VMEM((TOK, 128), f32),
            pltpu.VMEM((TOK, 128), f32),
            pltpu.SemaphoreType.DMA((n_keys,)),
            pltpu.SemaphoreType.DMA((n_keys,)),
            pltpu.SemaphoreType.DMA((n_keys,)),
            pltpu.SemaphoreType.DMA((n_keys,)),
            pltpu.SemaphoreType.DMA((10,)),
            pltpu.SemaphoreType.DMA((10,)),
            pltpu.SemaphoreType.DMA((2,)),
        ],
        compiler_params=pltpu.CompilerParams(
            collective_id=0, has_side_effects=True, vmem_limit_bytes=56 * 1024 * 1024
        ),
    )(
        cache_lengths,
        hidden[0],
        norm_gain.reshape(1, -1),
        jnp.asarray(inverse),
        w_query,
        w_key,
        w_value,
        w_out.T,
        cache_keys[0],
        cache_values[0],
    )
    return tuple(r[None] for r in results)


def solution(mesh):
    in_specs = (
        P("req", None, "tp"),
        P(),
        P("req", "tp"),
        P("req", "tp"),
        P("req", "tp"),
        P("tp", "req"),
        P("req", None, "tp"),
        P("req", None, "tp"),
        P(),
    )
    out_specs = (P("req", None, "tp"), P("req", None, "tp"), P("req", None, "tp"))
    return jax.shard_map(
        per_device, mesh=mesh, in_specs=in_specs, out_specs=out_specs, check_vma=False
    )
```

```python
import functools

import jax
import jax.numpy as jnp
import numpy as np
from jax import lax
from jax.experimental import pallas as pl
from jax.experimental.pallas import tpu as pltpu
from jax.sharding import PartitionSpec as P

HD = 64
NY, NZ, NX = 2, 8, 4
N_TP = 4
TOK = 128
ROW_BLOCKS = 4
HALF = TOK // 2

rope_base = 1000000.0
norm_eps = 1e-05
masked_score = -1e30
MESH = pl.DeviceIdType.MESH


def ring_keys(axis, n):
    keys = []
    for s in range(1, n // 2 + 1):
        for u in (0, 1):
            for d in (1, -1):
                if s < n // 2 or (u == 0) == (d == 1):
                    keys.append((axis, d, s, u))
    return keys


SIZE = {"x": NX, "z": NZ}
RING = {a: ring_keys(a, SIZE[a]) for a in SIZE}
DIRECT = {"x": [("direct", "x", k, u) for u in (0, 1) for k in (2, 1, 3)]}
STAGES = {0: ("x", "z"), 1: ("z", "x")}
HOPS = {0: {"z": {1: 1, 2: 2, 3: 1, 4: 2}}, 1: {"z": {1: 1, 2: 2, 3: 1, 4: 2}, "x": {1: 1, 2: 1}}}
ORDER = {"z": (2, 1, 3, 4), "x": (1, 2)}
FIRST = {"x": DIRECT["x"], "z": RING["z"]}
PASS = {c: [("own", 0), ("own", 1)] + RING[STAGES[c][1]] for c in (0, 1)}
KEYS = (
    [("local", 0), ("local", 1), ("core", 0), ("core", 1), "y"]
    + RING["x"]
    + RING["z"]
    + DIRECT["x"]
    + [("pass", c) + (k,) for c in (0, 1) for k in PASS[c]]
)
KEY_INDEX = {k: i for i, k in enumerate(KEYS)}


class Place:
    def __init__(self):
        req = lax.axis_index("req")
        self.tp = lax.axis_index("tp")
        self.core = lax.rem(req, 2)
        self.x = lax.rem(lax.div(req, 2), NX)
        self.z = lax.rem(lax.div(req, 2 * NX), NZ)
        self.y = lax.div(req, 2 * NX * NZ)

    def device(self, core=None, x=None, z=None, y=None, tp=None):
        core = self.core if core is None else core
        x = self.x if x is None else x
        z = self.z if z is None else z
        y = self.y if y is None else y
        tp = self.tp if tp is None else tp
        return (((y * NZ + z) * NX + x) * 2 + core, tp)

    def along(self, axis, offset):
        n = SIZE[axis]
        here = self.x if axis == "x" else self.z
        return lax.rem(here + (offset + 2 * n), n)


class Gather:
    def __init__(self, place, parts, buf, send, recv):
        self.place, self.parts, self.buf, self.send, self.recv = place, parts, buf, send, recv

    def first_block(self, c, u, axis, o):
        p = self.place
        yu = p.y if u == 0 else 1 - p.y
        return self.buf[c].at[yu, p.z, o] if axis == "x" else self.buf[c].at[yu, o, p.x]

    def second_block(self, c, u, axis, o):
        p = self.place
        yu = p.y if u == 0 else 1 - p.y
        return self.buf[c].at[yu, o] if axis == "z" else self.buf[c].at[yu, :, o]

    def make(self, c, key):
        p, i = self.place, KEY_INDEX[key]
        if key[0] == "local":
            src, column = self.parts[c][key[1]]
            columns = pl.ds(column, src.shape[1])
            dst = self.buf[c].at[p.y, p.z, p.x, pl.ds(c * 16, 16), columns]
            return pltpu.make_async_copy(src, dst, self.send.at[i])
        if key[0] == "core":
            src, column = self.parts[1 - c][key[1]]
            columns = pl.ds(column, src.shape[1])
            dst = self.buf[1 - c].at[p.y, p.z, p.x, pl.ds(c * 16, 16), columns]
            dev = p.device(core=1 - p.core)
        elif key == "y":
            src = dst = self.buf[c].at[p.y, p.z, p.x]
            dev = p.device(y=1 - p.y)
        elif key[0] == "pass":
            axis = STAGES[c][1]
            if key[2][0] == "own":
                u, o = key[2][1], p.along(axis, 0)
            else:
                _, d, s, u = key[2]
                o = p.along(axis, -d * s)
            src = dst = self.second_block(c, u, axis, o)
            dev = p.device(core=1 - p.core)
        elif key[0] == "direct":
            _, axis, k, u = key
            src = dst = self.first_block(c, u, axis, p.along(axis, 0))
            dev = p.device(**{axis: p.along(axis, k)})
        else:
            axis, d, s, u = key
            pick = self.first_block if axis == STAGES[c][0] else self.second_block
            hops = HOPS[c][axis][s]
            src = dst = pick(c, u, axis, p.along(axis, -d * (s - hops)))
            dev = p.device(**{axis: p.along(axis, d * hops)})
        return pltpu.make_async_remote_copy(
            src_ref=src,
            dst_ref=dst,
            send_sem=self.send.at[i],
            recv_sem=self.recv.at[i],
            device_id=dev,
            device_id_type=MESH,
        )

    def start(self, c, key):
        self.make(c, key).start()

    def land(self, c, key):
        self.make(c, key).wait_recv()

    def steps(self, c):
        first, second = STAGES[c]
        n_parts = range(len(self.parts[c]))

        def begin():
            for k in n_parts:
                self.start(c, ("core", k))
            for k in n_parts:
                self.start(c, ("local", k))

        def relay(axis, held, u, ways=(1, -1)):
            for s in ORDER[axis]:
                for d in ways:
                    if s - HOPS[c][axis][s] == held and (axis, d, s, u) in KEY_INDEX:
                        self.start(c, (axis, d, s, u))

        def start_first(u):
            if first == "z":
                relay(first, 0, u)
            else:
                for key in DIRECT[first]:
                    if key[3] == u:
                        self.start(c, key)

        def own():
            for k in n_parts:
                self.make(c, ("local", k)).wait()
                self.arrive(c, k)
            self.start(c, "y")
            start_first(0)

        def other():
            self.land(c, "y")
            start_first(1)

        def enter_second(u):
            relay(second, 0, u)
            self.start(c, ("pass", c, ("own", u)))

        def after_direct():
            for u in (0, 1):
                for key in DIRECT[first]:
                    if key[3] == u:
                        self.land(c, key)
                enter_second(u)

        def first_step(step):
            for key in RING[first]:
                _, d, s, u = key
                if s == step:
                    self.land(c, key)
                    relay(first, s, u, (d,))
                    if s == ORDER[first][-1]:
                        enter_second(u)

        def ring_step(keys):
            for key in keys:
                _, d, s, u = key
                self.land(c, key)
                relay(second, s, u, (d,))
                self.start(c, ("pass", c, key))

        def finish():
            for k in PASS[1 - c]:
                self.land(1 - c, ("pass", 1 - c, k))
            sent = [("core", k) for k in n_parts] + ["y"] + FIRST[first] + RING[second]
            for k in sent + [("pass", c, k) for k in PASS[c]]:
                self.make(c, k).wait_send()

        if first == "x":
            middle = [after_direct]
        else:
            middle = [functools.partial(first_step, i) for i in ORDER[first]]
        for i in ORDER[second]:
            middle.append(functools.partial(ring_step, [k for k in RING[second] if k[2] == i]))
        middle += [lambda: None] * (6 - len(middle))
        return [begin, own, other] + middle + [finish]

    def arrive(self, c, k):
        self.make(1 - c, ("core", k)).wait_recv()


def rotate(tile, cosine, sine, lane):
    partner = jnp.where((lane % 64) < 32, pltpu.roll(tile, 96, 1), pltpu.roll(tile, 32, 1))
    return tile * cosine + partner * sine


def kernel(
    lengths,
    hidden,
    gain,
    inverse,
    w_query,
    w_key,
    w_value,
    w_out,
    keys_far,
    values_far,
    out,
    new_keys,
    new_values,
    rows,
    keys,
    values,
    buf_in_0,
    buf_in_1,
    buf_out_0,
    buf_out_1,
    normed,
    queries,
    mixed_blocks,
    terms,
    landed,
    cosine,
    sine,
    send_in,
    recv_in,
    send_out,
    recv_out,
    send_tp,
    recv_tp,
    cache_sem,
):
    place = Place()
    cache_copies = [
        pltpu.make_async_copy(keys_far, keys, cache_sem.at[0]),
        pltpu.make_async_copy(values_far, values, cache_sem.at[1]),
    ]
    barrier = pltpu.get_barrier_semaphore()
    partners = [place.device(core=1 - place.core), place.device(y=1 - place.y)]
    for axis in ("x", "z"):
        partners += [
            place.device(**{axis: place.along(axis, k)})
            for k in range(1, SIZE[axis])
            if axis == "x" or min(k, SIZE[axis] - k) <= 2
        ]
    others = [lax.rem(place.tp + d, N_TP) for d in range(N_TP)]
    partners += [place.device(tp=others[d]) for d in range(1, N_TP)]
    for partner in partners:
        pl.semaphore_signal(barrier, inc=1, device_id=partner, device_id_type=MESH)
    for copy in cache_copies:
        copy.start()

    lane = lax.broadcasted_iota(jnp.int32, (TOK, 128), 1)
    position = lengths[lax.axis_index("req")] + lax.broadcasted_iota(jnp.int32, (TOK, 128), 0)
    phase = position.astype(jnp.float32) * inverse[...]
    cosine[...] = jnp.cos(phase)
    sine[...] = jnp.where((lane % 64) < 32, -1.0, 1.0) * jnp.sin(phase)

    pl.semaphore_wait(barrier, len(partners))

    parts_in = [
        [(w_query.at[:, pl.ds(256 * half, 256)], 0), ((w_key, w_value)[half], 256)]
        for half in (0, 1)
    ]
    parts_out = [[(w_out.at[:, pl.ds(256 * half, 256)], 0)] for half in (0, 1)]
    buf_in, buf_out = (buf_in_0, buf_in_1), (buf_out_0, buf_out_1)
    gather_in = Gather(place, parts_in, buf_in, send_in, recv_in)
    gather_out = Gather(place, parts_out, buf_out, send_out, recv_out)
    steps_in = {c: gather_in.steps(c) for c in (0, 1)}
    steps_out = {c: gather_out.steps(c) for c in (0, 1)}

    def run(steps, i):
        for c in (0, 1):
            pl.when(place.core == c)(steps[c][i])

    def hidden_copy(d):
        return pltpu.make_async_remote_copy(
            src_ref=hidden,
            dst_ref=rows.at[place.tp],
            send_sem=send_tp.at[d],
            recv_sem=recv_tp.at[d],
            device_id=place.device(tp=others[d]),
            device_id_type=MESH,
        )

    own_rows = pltpu.make_async_copy(hidden, rows.at[place.tp], send_tp.at[0])

    run(steps_in, 0)
    own_rows.start()
    run(steps_out, 0)
    run(steps_in, 1)
    run(steps_in, 2)
    run(steps_out, 1)
    for d in (2, 1, 3):
        hidden_copy(d).start()
    run(steps_in, 3)
    run(steps_out, 2)
    run(steps_in, 4)
    run(steps_out, 3)
    run(steps_in, 5)
    run(steps_out, 4)
    run(steps_in, 6)
    run(steps_out, 5)
    run(steps_in, 7)
    run(steps_out, 6)
    run(steps_in, 8)
    run(steps_out, 7)

    own_rows.wait()
    for d in (1, 2, 3):
        hidden_copy(d).wait()
    squares = 0.0
    for j in range(N_TP):
        part = rows[j].astype(jnp.float32)
        squares += jnp.sum(part * part, axis=-1, keepdims=True)
    scale = lax.rsqrt(squares * (1.0 / (512 * N_TP)) + norm_eps)
    for j in range(N_TP):
        part = rows[j].astype(jnp.float32)
        normed[j] = (part * scale * gain[:, 512 * j : 512 * (j + 1)].astype(jnp.float32)).astype(
            jnp.bfloat16
        )

    run(steps_in, 9)

    def project(c):
        total = jnp.zeros((TOK, 384), jnp.float32)
        for j in range(N_TP):
            block = buf_in[c][j // 2, 4 * (j % 2) : 4 * (j % 2) + 4].reshape(512, 384)
            total += jnp.dot(normed[j], block, preferred_element_type=jnp.float32)
        return total

    first, second = project(0), project(1)
    low = lane < 64
    cos_table, sin_table = cosine[...], sine[...]
    fresh_keys = rotate(first[:, 256:], cos_table, sin_table, lane).astype(jnp.bfloat16)
    fresh_values = second[:, 256:].astype(jnp.bfloat16)
    new_keys[...] = fresh_keys
    new_values[...] = fresh_values
    for g, half in enumerate((first, second)):
        for pair in range(2):
            tile = rotate(half[:, 128 * pair : 128 * pair + 128], cos_table, sin_table, lane)
            tile = tile.astype(jnp.bfloat16).astype(jnp.float32) * (HD**-0.5)
            swapped = pltpu.roll(tile, 64, 1)
            if g == 0:
                heads = (jnp.where(low, tile, 0.0), jnp.where(low, swapped, 0.0))
            else:
                heads = (jnp.where(low, 0.0, swapped), jnp.where(low, 0.0, tile))
            for k in range(2):
                head = heads[k].astype(jnp.bfloat16)
                row = HALF * (2 * pair + k)
                for t in range(2):
                    queries[2 * t + g, row : row + HALF, :] = head[HALF * t : HALF * (t + 1)]

    length = lengths[lax.axis_index("req")]
    slot = lax.broadcasted_iota(jnp.int32, (1, 2048), 1)
    cache_bias = jnp.where(slot < length, 0.0, masked_score)
    row_token = lax.broadcasted_iota(jnp.int32, (2 * TOK, TOK), 0) % HALF
    new_slot = lax.broadcasted_iota(jnp.int32, (2 * TOK, TOK), 1)
    contract_last = (((1,), (1,)), ((), ()))

    def attend(i, carry):
        pl.when(i == 0)(lambda: run(steps_out, 8))
        block = queries[i]
        cache_scores = (
            lax.dot_general(block, keys[...], contract_last, preferred_element_type=jnp.float32)
            + cache_bias
        )
        new_scores = (
            lax.dot_general(
                block, new_keys[...], contract_last, preferred_element_type=jnp.float32
            )
            + jnp.where(new_slot <= row_token + HALF * lax.div(i, 2), 0.0, masked_score)
        )
        peak = jnp.maximum(
            jnp.max(cache_scores, axis=-1, keepdims=True),
            jnp.max(new_scores, axis=-1, keepdims=True),
        )
        cache_weights = jnp.exp(cache_scores - peak)
        new_weights = jnp.exp(new_scores - peak)
        total = jnp.sum(cache_weights, axis=-1, keepdims=True) + jnp.sum(
            new_weights, axis=-1, keepdims=True
        )
        mixed = jnp.dot(
            cache_weights.astype(jnp.bfloat16), values[...], preferred_element_type=jnp.float32
        ) + jnp.dot(
            new_weights.astype(jnp.bfloat16), new_values[...], preferred_element_type=jnp.float32
        )
        mixed_blocks[i] = mixed / total
        return carry

    for copy in cache_copies:
        copy.wait()
    low = lax.broadcasted_iota(jnp.int32, (HALF, 128), 1) < 64

    def mixed_rows(t):
        tiles = []
        for g in range(2):
            for pair in range(2):
                row = 2 * HALF * pair
                even = mixed_blocks[2 * t + g, row : row + HALF, :]
                odd = mixed_blocks[2 * t + g, row + HALF : row + 2 * HALF, :]
                if g == 0:
                    tile = jnp.where(low, even, pltpu.roll(odd, 64, 1))
                else:
                    tile = jnp.where(low, pltpu.roll(even, 64, 1), odd)
                tiles.append(tile.astype(jnp.bfloat16))
        return jnp.concatenate(tiles[:2], axis=1), jnp.concatenate(tiles[2:], axis=1)

    def term_copy(t, d):
        return pltpu.make_async_remote_copy(
            src_ref=terms.at[d - 1, pl.ds(HALF * t, HALF)],
            dst_ref=landed.at[d - 1, pl.ds(HALF * t, HALF)],
            send_sem=send_tp.at[1 + 3 * (t + 1) + d - 1],
            recv_sem=recv_tp.at[1 + 3 * (t + 1) + d - 1],
            device_id=place.device(tp=others[d]),
            device_id_type=MESH,
        )

    def term(shares, d):
        target = others[d]
        total = jnp.zeros((HALF, 512), jnp.float32)
        for c in range(2):
            block = buf_out[c][lax.div(target, 2), pl.ds(4 * lax.rem(target, 2), 4)]
            total += lax.dot_general(
                shares[c],
                block.reshape(512, block.shape[-1]),
                contract_last,
                preferred_element_type=jnp.float32,
            )
        return total.astype(jnp.bfloat16)

    own_terms = []
    for t in range(2):
        lax.fori_loop(2 * t, 2 * t + 2, attend, 0)
        if t == 0:
            run(steps_out, 9)
        shares = mixed_rows(t)
        for d in (2, 1, 3):
            terms[d - 1, HALF * t : HALF * (t + 1), :] = term(shares, d)
            term_copy(t, d).start()
        own_terms.append(term(shares, 0).astype(jnp.float32))
    for t in range(2):
        summed = own_terms[t]
        for d in (1, 3, 2):
            term_copy(t, d).wait()
            summed += landed[d - 1, HALF * t : HALF * (t + 1), :].astype(jnp.float32)
        out[HALF * t : HALF * (t + 1), :] = summed.astype(jnp.bfloat16)


def per_device(
    hidden, norm_gain, w_query, w_key, w_value, w_out, cache_keys, cache_values, cache_lengths
):
    powers = np.arange(0, HD, 2, dtype=np.float64) / HD
    inverse = np.tile((rope_base**-powers).astype(np.float32), 4).reshape(1, 128)
    vmem = pl.BlockSpec(memory_space=pltpu.VMEM)
    far = pl.BlockSpec(memory_space=pl.ANY)
    bf16, f32 = jnp.bfloat16, jnp.float32
    n_keys = len(KEYS)
    results = pl.pallas_call(
        kernel,
        out_shape=(
            jax.ShapeDtypeStruct((TOK, 512), bf16),
            jax.ShapeDtypeStruct((TOK, 128), bf16),
            jax.ShapeDtypeStruct((TOK, 128), bf16),
        ),
        in_specs=[pl.BlockSpec(memory_space=pltpu.SMEM), far, vmem, vmem] + [far] * 6,
        out_specs=(vmem, vmem, vmem),
        scratch_shapes=[
            pltpu.VMEM((N_TP, TOK, 512), bf16),
            pltpu.VMEM((2048, 128), bf16),
            pltpu.VMEM((2048, 128), bf16),
            pltpu.VMEM((NY, NZ, NX, 32, 384), bf16),
            pltpu.VMEM((NY, NZ, NX, 32, 384), bf16),
            pltpu.VMEM((NY, NZ, NX, 32, 256), bf16),
            pltpu.VMEM((NY, NZ, NX, 32, 256), bf16),
            pltpu.VMEM((N_TP, TOK, 512), bf16),
            pltpu.VMEM((ROW_BLOCKS, 2 * TOK, 128), bf16),
            pltpu.VMEM((ROW_BLOCKS, 2 * TOK, 128), f32),
            pltpu.VMEM((N_TP - 1, TOK, 512), bf16),
            pltpu.VMEM((N_TP - 1, TOK, 512), bf16),
            pltpu.VMEM((TOK, 128), f32),
            pltpu.VMEM((TOK, 128), f32),
            pltpu.SemaphoreType.DMA((n_keys,)),
            pltpu.SemaphoreType.DMA((n_keys,)),
            pltpu.SemaphoreType.DMA((n_keys,)),
            pltpu.SemaphoreType.DMA((n_keys,)),
            pltpu.SemaphoreType.DMA((10,)),
            pltpu.SemaphoreType.DMA((10,)),
            pltpu.SemaphoreType.DMA((2,)),
        ],
        compiler_params=pltpu.CompilerParams(
            collective_id=0, has_side_effects=True, vmem_limit_bytes=56 * 1024 * 1024
        ),
    )(
        cache_lengths,
        hidden[0],
        norm_gain.reshape(1, -1),
        jnp.asarray(inverse),
        w_query,
        w_key,
        w_value,
        w_out.T,
        cache_keys[0],
        cache_values[0],
    )
    return tuple(r[None] for r in results)


def solution(mesh):
    in_specs = (
        P("req", None, "tp"),
        P(),
        P("req", "tp"),
        P("req", "tp"),
        P("req", "tp"),
        P("tp", "req"),
        P("req", None, "tp"),
        P("req", None, "tp"),
        P(),
    )
    out_specs = (P("req", None, "tp"), P("req", None, "tp"), P("req", None, "tp"))
    return jax.shard_map(
        per_device, mesh=mesh, in_specs=in_specs, out_specs=out_specs, check_vma=False
    )
```

```python
import functools

import jax
import jax.numpy as jnp
import numpy as np
from jax import lax
from jax.experimental import pallas as pl
from jax.experimental.pallas import tpu as pltpu
from jax.sharding import PartitionSpec as P

HD = 64
NY, NZ, NX = 2, 8, 4
N_TP = 4
TOK = 128
ROW_BLOCKS = 4
HALF = TOK // 2

rope_base = 1000000.0
norm_eps = 1e-05
masked_score = -1e30
MESH = pl.DeviceIdType.MESH


def ring_keys(axis, n):
    keys = []
    for s in range(1, n // 2 + 1):
        for u in (0, 1):
            for d in (1, -1):
                if s < n // 2 or (u == 0) == (d == 1):
                    keys.append((axis, d, s, u))
    return keys


SIZE = {"x": NX, "z": NZ}
RING = {a: ring_keys(a, SIZE[a]) for a in SIZE}
DIRECT = {"x": [("direct", "x", k, u) for u in (0, 1) for k in (2, 1, 3)]}
STAGES = {0: ("x", "z"), 1: ("z", "x")}
HOPS = {0: {"z": {1: 1, 2: 2, 3: 1, 4: 2}}, 1: {"z": {1: 1, 2: 2, 3: 1, 4: 2}, "x": {1: 1, 2: 1}}}
ORDER = {"z": (2, 1, 3, 4), "x": (1, 2)}
FIRST = {"x": DIRECT["x"], "z": RING["z"]}
PASS = {c: [("own", 0), ("own", 1)] + RING[STAGES[c][1]] for c in (0, 1)}
KEYS = (
    [("local", 0), ("local", 1), ("core", 0), ("core", 1), "y"]
    + RING["x"]
    + RING["z"]
    + DIRECT["x"]
    + [("pass", c) + (k,) for c in (0, 1) for k in PASS[c]]
)
KEY_INDEX = {k: i for i, k in enumerate(KEYS)}


class Place:
    def __init__(self):
        req = lax.axis_index("req")
        self.tp = lax.axis_index("tp")
        self.core = lax.rem(req, 2)
        self.x = lax.rem(lax.div(req, 2), NX)
        self.z = lax.rem(lax.div(req, 2 * NX), NZ)
        self.y = lax.div(req, 2 * NX * NZ)

    def device(self, core=None, x=None, z=None, y=None, tp=None):
        core = self.core if core is None else core
        x = self.x if x is None else x
        z = self.z if z is None else z
        y = self.y if y is None else y
        tp = self.tp if tp is None else tp
        return (((y * NZ + z) * NX + x) * 2 + core, tp)

    def along(self, axis, offset):
        n = SIZE[axis]
        here = self.x if axis == "x" else self.z
        return lax.rem(here + (offset + 2 * n), n)


class Gather:
    def __init__(self, place, parts, buf, send, recv):
        self.place, self.parts, self.buf, self.send, self.recv = place, parts, buf, send, recv

    def first_block(self, c, u, axis, o):
        p = self.place
        yu = p.y if u == 0 else 1 - p.y
        return self.buf[c].at[yu, p.z, o] if axis == "x" else self.buf[c].at[yu, o, p.x]

    def second_block(self, c, u, axis, o):
        p = self.place
        yu = p.y if u == 0 else 1 - p.y
        return self.buf[c].at[yu, o] if axis == "z" else self.buf[c].at[yu, :, o]

    def make(self, c, key):
        p, i = self.place, KEY_INDEX[key]
        if key[0] == "local":
            src, column = self.parts[c][key[1]]
            columns = pl.ds(column, src.shape[1])
            dst = self.buf[c].at[p.y, p.z, p.x, pl.ds(c * 16, 16), columns]
            return pltpu.make_async_copy(src, dst, self.send.at[i])
        if key[0] == "core":
            src, column = self.parts[1 - c][key[1]]
            columns = pl.ds(column, src.shape[1])
            dst = self.buf[1 - c].at[p.y, p.z, p.x, pl.ds(c * 16, 16), columns]
            dev = p.device(core=1 - p.core)
        elif key == "y":
            src = dst = self.buf[c].at[p.y, p.z, p.x]
            dev = p.device(y=1 - p.y)
        elif key[0] == "pass":
            axis = STAGES[c][1]
            if key[2][0] == "own":
                u, o = key[2][1], p.along(axis, 0)
            else:
                _, d, s, u = key[2]
                o = p.along(axis, -d * s)
            src = dst = self.second_block(c, u, axis, o)
            dev = p.device(core=1 - p.core)
        elif key[0] == "direct":
            _, axis, k, u = key
            src = dst = self.first_block(c, u, axis, p.along(axis, 0))
            dev = p.device(**{axis: p.along(axis, k)})
        else:
            axis, d, s, u = key
            pick = self.first_block if axis == STAGES[c][0] else self.second_block
            hops = HOPS[c][axis][s]
            src = dst = pick(c, u, axis, p.along(axis, -d * (s - hops)))
            dev = p.device(**{axis: p.along(axis, d * hops)})
        return pltpu.make_async_remote_copy(
            src_ref=src,
            dst_ref=dst,
            send_sem=self.send.at[i],
            recv_sem=self.recv.at[i],
            device_id=dev,
            device_id_type=MESH,
        )

    def start(self, c, key):
        self.make(c, key).start()

    def land(self, c, key):
        self.make(c, key).wait_recv()

    def steps(self, c):
        first, second = STAGES[c]
        n_parts = range(len(self.parts[c]))

        def begin():
            for k in n_parts:
                self.start(c, ("core", k))
            for k in n_parts:
                self.start(c, ("local", k))

        def relay(axis, held, u, ways=(1, -1)):
            for s in ORDER[axis]:
                for d in ways:
                    if s - HOPS[c][axis][s] == held and (axis, d, s, u) in KEY_INDEX:
                        self.start(c, (axis, d, s, u))

        def start_first(u):
            if first == "z":
                relay(first, 0, u)
            else:
                for key in DIRECT[first]:
                    if key[3] == u:
                        self.start(c, key)

        def own():
            for k in n_parts:
                self.make(c, ("local", k)).wait()
                self.arrive(c, k)
            self.start(c, "y")
            start_first(0)

        def other():
            self.land(c, "y")
            start_first(1)

        def enter_second(u):
            relay(second, 0, u)
            self.start(c, ("pass", c, ("own", u)))

        def after_direct():
            for u in (0, 1):
                for key in DIRECT[first]:
                    if key[3] == u:
                        self.land(c, key)
                enter_second(u)

        def first_step(step):
            for key in RING[first]:
                _, d, s, u = key
                if s == step:
                    self.land(c, key)
                    relay(first, s, u, (d,))
                    if s == ORDER[first][-1]:
                        enter_second(u)

        def ring_step(keys):
            for key in keys:
                _, d, s, u = key
                self.land(c, key)
                relay(second, s, u, (d,))
                self.start(c, ("pass", c, key))

        def finish():
            for k in PASS[1 - c]:
                self.land(1 - c, ("pass", 1 - c, k))
            sent = [("core", k) for k in n_parts] + ["y"] + FIRST[first] + RING[second]
            for k in sent + [("pass", c, k) for k in PASS[c]]:
                self.make(c, k).wait_send()

        if first == "x":
            middle = [after_direct]
        else:
            middle = [functools.partial(first_step, i) for i in ORDER[first]]
        for i in ORDER[second]:
            middle.append(functools.partial(ring_step, [k for k in RING[second] if k[2] == i]))
        middle += [lambda: None] * (6 - len(middle))
        return [begin, own, other] + middle + [finish]

    def arrive(self, c, k):
        self.make(1 - c, ("core", k)).wait_recv()


def rotate(tile, cosine, sine, lane):
    partner = jnp.where((lane % 64) < 32, pltpu.roll(tile, 96, 1), pltpu.roll(tile, 32, 1))
    return tile * cosine + partner * sine


def kernel(
    lengths,
    hidden,
    gain,
    inverse,
    w_query,
    w_key,
    w_value,
    w_out,
    keys_far,
    values_far,
    out,
    new_keys,
    new_values,
    rows,
    keys,
    values,
    buf_in_0,
    buf_in_1,
    buf_out_0,
    buf_out_1,
    normed,
    queries,
    mixed_blocks,
    terms,
    landed,
    cosine,
    sine,
    send_in,
    recv_in,
    send_out,
    recv_out,
    send_tp,
    recv_tp,
    cache_sem,
):
    place = Place()
    cache_copies = [
        pltpu.make_async_copy(keys_far, keys, cache_sem.at[0]),
        pltpu.make_async_copy(values_far, values, cache_sem.at[1]),
    ]
    barrier = pltpu.get_barrier_semaphore()
    partners = [place.device(core=1 - place.core), place.device(y=1 - place.y)]
    for axis in ("x", "z"):
        partners += [
            place.device(**{axis: place.along(axis, k)})
            for k in range(1, SIZE[axis])
            if axis == "x" or min(k, SIZE[axis] - k) <= 2
        ]
    others = [lax.rem(place.tp + d, N_TP) for d in range(N_TP)]
    partners += [place.device(tp=others[d]) for d in range(1, N_TP)]
    for partner in partners:
        pl.semaphore_signal(barrier, inc=1, device_id=partner, device_id_type=MESH)
    for copy in cache_copies:
        copy.start()

    lane = lax.broadcasted_iota(jnp.int32, (TOK, 128), 1)
    position = lengths[lax.axis_index("req")] + lax.broadcasted_iota(jnp.int32, (TOK, 128), 0)
    phase = position.astype(jnp.float32) * inverse[...]
    cosine[...] = jnp.cos(phase)
    sine[...] = jnp.where((lane % 64) < 32, -1.0, 1.0) * jnp.sin(phase)

    pl.semaphore_wait(barrier, len(partners))

    parts_in = [
        [(w_query.at[:, pl.ds(256 * half, 256)], 0), ((w_key, w_value)[half], 256)]
        for half in (0, 1)
    ]
    parts_out = [[(w_out.at[:, pl.ds(256 * half, 256)], 0)] for half in (0, 1)]
    buf_in, buf_out = (buf_in_0, buf_in_1), (buf_out_0, buf_out_1)
    gather_in = Gather(place, parts_in, buf_in, send_in, recv_in)
    gather_out = Gather(place, parts_out, buf_out, send_out, recv_out)
    steps_in = {c: gather_in.steps(c) for c in (0, 1)}
    steps_out = {c: gather_out.steps(c) for c in (0, 1)}

    def run(steps, i):
        for c in (0, 1):
            pl.when(place.core == c)(steps[c][i])

    def hidden_copy(d):
        return pltpu.make_async_remote_copy(
            src_ref=hidden,
            dst_ref=rows.at[place.tp],
            send_sem=send_tp.at[d],
            recv_sem=recv_tp.at[d],
            device_id=place.device(tp=others[d]),
            device_id_type=MESH,
        )

    own_rows = pltpu.make_async_copy(hidden, rows.at[place.tp], send_tp.at[0])

    run(steps_in, 0)
    own_rows.start()
    run(steps_out, 0)
    run(steps_in, 1)
    run(steps_in, 2)
    run(steps_out, 1)
    for d in (2, 1, 3):
        hidden_copy(d).start()
    run(steps_in, 3)
    run(steps_out, 2)
    run(steps_in, 4)
    run(steps_out, 3)
    run(steps_in, 5)
    run(steps_out, 4)
    run(steps_in, 6)
    run(steps_out, 5)
    run(steps_in, 7)
    run(steps_out, 6)
    run(steps_in, 8)
    run(steps_out, 7)

    own_rows.wait()
    for d in (1, 2, 3):
        hidden_copy(d).wait()
    gain_row = gain[...].astype(jnp.float32).reshape(1, 512 * N_TP)
    squares = 0.0
    for j in range(N_TP):
        part = rows[j].astype(jnp.float32)
        squares += jnp.sum(part * part, axis=-1, keepdims=True)
    scale = lax.rsqrt(squares * (1.0 / (512 * N_TP)) + norm_eps)
    for j in range(N_TP):
        part = rows[j].astype(jnp.float32)
        normed[j] = (part * scale * gain_row[:, 512 * j : 512 * (j + 1)]).astype(
            jnp.bfloat16
        )

    run(steps_in, 9)

    def project(c):
        total = jnp.zeros((TOK, 384), jnp.float32)
        for j in range(N_TP):
            block = buf_in[c][j // 2, 4 * (j % 2) : 4 * (j % 2) + 4].reshape(512, 384)
            total += jnp.dot(normed[j], block, preferred_element_type=jnp.float32)
        return total

    first, second = project(0), project(1)
    low = lane < 64
    cos_table, sin_table = cosine[...], sine[...]
    fresh_keys = rotate(first[:, 256:], cos_table, sin_table, lane).astype(jnp.bfloat16)
    fresh_values = second[:, 256:].astype(jnp.bfloat16)
    new_keys[...] = fresh_keys
    new_values[...] = fresh_values
    for g, half in enumerate((first, second)):
        for pair in range(2):
            tile = rotate(half[:, 128 * pair : 128 * pair + 128], cos_table, sin_table, lane)
            tile = tile.astype(jnp.bfloat16).astype(jnp.float32) * (HD**-0.5)
            swapped = pltpu.roll(tile, 64, 1)
            if g == 0:
                heads = (jnp.where(low, tile, 0.0), jnp.where(low, swapped, 0.0))
            else:
                heads = (jnp.where(low, 0.0, swapped), jnp.where(low, 0.0, tile))
            for k in range(2):
                head = heads[k].astype(jnp.bfloat16)
                row = HALF * (2 * pair + k)
                for t in range(2):
                    queries[2 * t + g, row : row + HALF, :] = head[HALF * t : HALF * (t + 1)]

    length = lengths[lax.axis_index("req")]
    slot = lax.broadcasted_iota(jnp.int32, (1, 2048), 1)
    cache_bias = jnp.where(slot < length, 0.0, masked_score)
    row_token = lax.broadcasted_iota(jnp.int32, (2 * TOK, TOK), 0) % HALF
    new_slot = lax.broadcasted_iota(jnp.int32, (2 * TOK, TOK), 1)
    contract_last = (((1,), (1,)), ((), ()))

    def attend(i, carry):
        pl.when(i == 0)(lambda: run(steps_out, 8))
        block = queries[i]
        cache_scores = (
            lax.dot_general(block, keys[...], contract_last, preferred_element_type=jnp.float32)
            + cache_bias
        )
        new_scores = (
            lax.dot_general(
                block, new_keys[...], contract_last, preferred_element_type=jnp.float32
            )
            + jnp.where(new_slot <= row_token + HALF * lax.div(i, 2), 0.0, masked_score)
        )
        peak = jnp.maximum(
            jnp.max(cache_scores, axis=-1, keepdims=True),
            jnp.max(new_scores, axis=-1, keepdims=True),
        )
        cache_weights = jnp.exp(cache_scores - peak)
        new_weights = jnp.exp(new_scores - peak)
        total = jnp.sum(cache_weights, axis=-1, keepdims=True) + jnp.sum(
            new_weights, axis=-1, keepdims=True
        )
        mixed = jnp.dot(
            cache_weights.astype(jnp.bfloat16), values[...], preferred_element_type=jnp.float32
        ) + jnp.dot(
            new_weights.astype(jnp.bfloat16), new_values[...], preferred_element_type=jnp.float32
        )
        mixed_blocks[i] = mixed / total
        return carry

    for copy in cache_copies:
        copy.wait()
    low = lax.broadcasted_iota(jnp.int32, (HALF, 128), 1) < 64

    def mixed_rows(t):
        tiles = []
        for g in range(2):
            for pair in range(2):
                row = 2 * HALF * pair
                even = mixed_blocks[2 * t + g, row : row + HALF, :]
                odd = mixed_blocks[2 * t + g, row + HALF : row + 2 * HALF, :]
                if g == 0:
                    tile = jnp.where(low, even, pltpu.roll(odd, 64, 1))
                else:
                    tile = jnp.where(low, pltpu.roll(even, 64, 1), odd)
                tiles.append(tile.astype(jnp.bfloat16))
        return jnp.concatenate(tiles[:2], axis=1), jnp.concatenate(tiles[2:], axis=1)

    def term_copy(t, d):
        return pltpu.make_async_remote_copy(
            src_ref=terms.at[d - 1, pl.ds(HALF * t, HALF)],
            dst_ref=landed.at[d - 1, pl.ds(HALF * t, HALF)],
            send_sem=send_tp.at[1 + 3 * (t + 1) + d - 1],
            recv_sem=recv_tp.at[1 + 3 * (t + 1) + d - 1],
            device_id=place.device(tp=others[d]),
            device_id_type=MESH,
        )

    def term(shares, d):
        target = others[d]
        total = jnp.zeros((HALF, 512), jnp.float32)
        for c in range(2):
            block = buf_out[c][lax.div(target, 2), pl.ds(4 * lax.rem(target, 2), 4)]
            total += lax.dot_general(
                shares[c],
                block.reshape(512, block.shape[-1]),
                contract_last,
                preferred_element_type=jnp.float32,
            )
        return total.astype(jnp.bfloat16)

    own_terms = []
    for t in range(2):
        lax.fori_loop(2 * t, 2 * t + 2, attend, 0)
        if t == 0:
            run(steps_out, 9)
        shares = mixed_rows(t)
        for d in (2, 1, 3):
            terms[d - 1, HALF * t : HALF * (t + 1), :] = term(shares, d)
            term_copy(t, d).start()
        own_terms.append(term(shares, 0).astype(jnp.float32))
    for t in range(2):
        summed = own_terms[t]
        for d in (1, 3, 2):
            term_copy(t, d).wait()
            summed += landed[d - 1, HALF * t : HALF * (t + 1), :].astype(jnp.float32)
        out[HALF * t : HALF * (t + 1), :] = summed.astype(jnp.bfloat16)


def per_device(
    hidden, norm_gain, w_query, w_key, w_value, w_out, cache_keys, cache_values, cache_lengths
):
    powers = np.arange(0, HD, 2, dtype=np.float64) / HD
    inverse = np.tile((rope_base**-powers).astype(np.float32), 4).reshape(1, 128)
    vmem = pl.BlockSpec(memory_space=pltpu.VMEM)
    far = pl.BlockSpec(memory_space=pl.ANY)
    bf16, f32 = jnp.bfloat16, jnp.float32
    n_keys = len(KEYS)
    results = pl.pallas_call(
        kernel,
        out_shape=(
            jax.ShapeDtypeStruct((TOK, 512), bf16),
            jax.ShapeDtypeStruct((TOK, 128), bf16),
            jax.ShapeDtypeStruct((TOK, 128), bf16),
        ),
        in_specs=[pl.BlockSpec(memory_space=pltpu.SMEM), far, vmem, vmem] + [far] * 6,
        out_specs=(vmem, vmem, vmem),
        scratch_shapes=[
            pltpu.VMEM((N_TP, TOK, 512), bf16),
            pltpu.VMEM((2048, 128), bf16),
            pltpu.VMEM((2048, 128), bf16),
            pltpu.VMEM((NY, NZ, NX, 32, 384), bf16),
            pltpu.VMEM((NY, NZ, NX, 32, 384), bf16),
            pltpu.VMEM((NY, NZ, NX, 32, 256), bf16),
            pltpu.VMEM((NY, NZ, NX, 32, 256), bf16),
            pltpu.VMEM((N_TP, TOK, 512), bf16),
            pltpu.VMEM((ROW_BLOCKS, 2 * TOK, 128), bf16),
            pltpu.VMEM((ROW_BLOCKS, 2 * TOK, 128), f32),
            pltpu.VMEM((N_TP - 1, TOK, 512), bf16),
            pltpu.VMEM((N_TP - 1, TOK, 512), bf16),
            pltpu.VMEM((TOK, 128), f32),
            pltpu.VMEM((TOK, 128), f32),
            pltpu.SemaphoreType.DMA((n_keys,)),
            pltpu.SemaphoreType.DMA((n_keys,)),
            pltpu.SemaphoreType.DMA((n_keys,)),
            pltpu.SemaphoreType.DMA((n_keys,)),
            pltpu.SemaphoreType.DMA((10,)),
            pltpu.SemaphoreType.DMA((10,)),
            pltpu.SemaphoreType.DMA((2,)),
        ],
        compiler_params=pltpu.CompilerParams(
            collective_id=0, has_side_effects=True, vmem_limit_bytes=56 * 1024 * 1024
        ),
    )(
        cache_lengths,
        hidden[0],
        norm_gain,
        jnp.asarray(inverse),
        w_query,
        w_key,
        w_value,
        w_out.T,
        cache_keys[0],
        cache_values[0],
    )
    return tuple(r[None] for r in results)


def solution(mesh):
    in_specs = (
        P("req", None, "tp"),
        P(),
        P("req", "tp"),
        P("req", "tp"),
        P("req", "tp"),
        P("tp", "req"),
        P("req", None, "tp"),
        P("req", None, "tp"),
        P(),
    )
    out_specs = (P("req", None, "tp"), P("req", None, "tp"), P("req", None, "tp"))
    return jax.shard_map(
        per_device, mesh=mesh, in_specs=in_specs, out_specs=out_specs, check_vma=False
    )
```
